32 devices in a mesh: sec: 2 (over core), tile: 16 (over z, y, x).
Axes of the slice: x: 2, y: 2, z: 4, core: 2. Of those that a mesh axis runs over, the one named last changes fastest.
Arguments:
- atm_state: bfloat16 [32768, 1024], P(('sec', 'tile')), may hold values from -6 to 6
- gain_atm: float32 [1024], replicated, may hold values from 0.25 to 1.75
- w_up_atm: bfloat16 [1024, 2048], replicated, may hold values from -0.1875 to 0.1875
- w_down_atm: bfloat16 [2048, 1024], replicated, may hold values from -0.125 to 0.125
- w_flux: bfloat16 [1024, 128], replicated, may hold values from -0.1875 to 0.1875
- ent_source: int32 [4096], P(('sec', 'tile')), may hold values from 0 to 7
- ent_target: int32 [4096, 1], P(('sec', 'tile')), may hold values from 0 to 31; in each aligned block of 128 rows (0 to 127, 128 to 255, ...) at most 8 rows name the same one
- ent_block: int32 [4096], P(('sec', 'tile')), may hold values from 0 to 44
- remap_weights: bfloat16 [4096, 128, 128], P(('sec', 'tile')), may hold values from -0.5 to 0.5
- ocean_state: bfloat16 [200, 184320], P(None, ('sec', 'tile')), may hold values from -6 to 6
- land_sea: int32 [184320], P(('sec', 'tile')), may hold values 0 or 1
- conv_kernel: float32 [200, 9], replicated, may hold values from -2.5 to 2.5
- w_force: bfloat16 [128, 200], replicated, may hold values from -0.5 to 0.5
- gain_ocn: float32 [200], replicated, may hold values from 0.25 to 1.75
- w_up_ocn: bfloat16 [200, 800], replicated, may hold values from -0.4375 to 0.4375
- w_down_ocn: bfloat16 [800, 200], replicated, may hold values from -0.21875 to 0.21875
Outputs:
- atm_next: bfloat16 [32768, 1024], P(('sec', 'tile'))
- ocean_next: bfloat16 [200, 184320], P(None, ('sec', 'tile'))
The draws below stay inside these ranges and needn't reach their ends.
Inputs may be any that keep to these rules, and one draw needn't show every extreme that they name: `ent_target`: among the 128 entries of one device no ocean tile is named more than 8 times, a bound that some block reaches; every tile is named by some entry.
All inputs are finite; a program needn't handle non-finite values. No bound on the sum of `land_sea` on one device may be relied on, other than what follows from the above.
Results may differ from the reference program's by a relative error of at most 0.009.
Values may be sent and summed in bfloat16 or wider, within the bound.
No kernel may reach another device: no remote copies, remote signals or barrier semaphores. Data moves between devices by JAX's collectives and lax.ppermute only.
A program may use at most 192 MiB of HBM per device.

```python
import math
import jax
import jax.numpy as jnp
import numpy as np
from jax import lax

DA = 1024
HA = 2048
FX = 128
DO = 200
HO = 800
OX = 1440
BLK = 128
OY = 4
C_ATM = 1024
ENT_DEV = 128
TILES = 32
CAP = 8
NB_ATM = 8
NB_OCN = 45
ACOLS = 32768
OCELLS = 184320
ENTRIES = 4096
N_SEC = 2
N_TILE = 16


def with_ends(array, own_key, least, largest):
    place = [jax.random.randint(jax.random.fold_in(own_key, axis), (), 0, length) for axis, length in enumerate(array.shape)]
    main_axis = array.shape.index(max(array.shape))
    beside = place[:main_axis] + [(place[main_axis] + 1) % array.shape[main_axis]] + place[main_axis + 1:]
    return array.at[tuple(place)].set(least).at[tuple(beside)].set(largest)


def steps_of(rng, extent, pieces, least, high):
    loudness = 1.0
    for position, shards_of in pieces:
        draws = jax.random.uniform(jax.random.fold_in(jax.random.fold_in(rng, 6), position), (shards_of,), jnp.float32, least / len(pieces), high / len(pieces))
        loudness = loudness * jnp.repeat(jnp.exp(draws), extent[position] // shards_of).reshape((-1,) + (1,) * (len(extent) - 1 - position))
    return loudness


def shared_out(key, own, number, rows, amount, top, most, skew):
    order = jax.random.permutation(key, amount)
    crowded, usual = shares(amount, rows * top, most, skew, True), shares(amount, rows * top, most, skew, False)
    places = jnp.arange(amount)

    def named(tallies, rotation):
        used = int((tallies > 0).sum())
        fixed = max(1, used // 4)
        moved = fixed + (places - fixed + rotation * (used - fixed)) % max(1, amount - fixed)
        return jnp.zeros((amount,), jnp.int32).at[order[jnp.where(places < fixed, places, moved)]].set(jnp.asarray(tallies, jnp.int32))

    tallies = jnp.where(number % 4 == 0, named(crowded, number // 4), named(usual, number - number // 4 - 1))
    mixed = jax.random.permutation(jax.random.fold_in(own, 3), amount)
    giver, taker = mixed[0:amount // 2 * 2:2], mixed[1:amount // 2 * 2:2]
    slack = jnp.minimum(tallies[giver] - 1, most - tallies[taker]) // 2
    slack = jnp.where((giver == order[0]) | (taker == order[0]) | (tallies[taker] == 0), 0, jnp.maximum(slack, 0))
    moved = jax.random.randint(jax.random.fold_in(own, 4), (amount // 2,), 0, 1 << 20) % (slack + 1)
    tallies = tallies.at[giver].add(-moved).at[taker].add(moved)
    members = jnp.searchsorted(jnp.cumsum(tallies), jnp.arange(rows * top), side="right").astype(jnp.int32)
    table = members.reshape(top, rows).T
    table = table[jax.random.permutation(jax.random.fold_in(own, 1), rows)]
    rotation = jax.random.randint(jax.random.fold_in(own, 2), (rows, 1), 0, top)
    return jnp.take_along_axis(table, (jnp.arange(top)[None, :] + rotation) % top, axis=1)


def shares(number_of, total, limit, slope, full):
    weights = [(1 << 20) // math.isqrt(rank ** slope) + 1 for rank in range(1, number_of + 1)]
    largest = limit if full else min(limit, max(-(-total // number_of), total * weights[0] // sum(weights)))
    least = 1 if total - largest >= number_of - 1 else 0
    counts, spare = [largest] + [least] * (number_of - 1), total - largest - least * (number_of - 1)
    while spare > 0:
        movable = [i for i in range(1, number_of) if counts[i] < largest] or [i for i in range(1, number_of) if counts[i] < limit]
        mass, remaining = sum([weights[i] for i in movable]), spare
        for i in movable:
            extra = min(limit - counts[i], max(1, remaining * weights[i] // mass), spare)
            counts[i] = counts[i] + extra
            spare = spare - extra
    return np.array(counts)


def gaussian(own_key, dims, spread, limit, pieces=(), kind=jnp.bfloat16):
    values = spread * jax.random.normal(own_key, dims, jnp.float32)
    if pieces:
        values = values * steps_of(own_key, dims, pieces, -0.22, 0.18)
    return jnp.clip(values, -limit, limit).astype(kind)


def setup_inputs(seed: int = 0) -> dict:
    arg_keys = jax.random.split(jax.random.key(seed), 17)
    atm_state = gaussian(arg_keys[0], (ACOLS, DA), 1.0, 6.0, ((0, 32),))
    gain_atm = jnp.clip(1.0 + 0.15 * jax.random.normal(arg_keys[1], (DA,), jnp.float32), 0.25, 1.75)
    w_up_atm = gaussian(arg_keys[2], (DA, HA), DA ** -0.5, 0.1875)
    w_down_atm = gaussian(arg_keys[3], (HA, DA), HA ** -0.5, 0.125)
    w_flux = gaussian(arg_keys[4], (DA, FX), DA ** -0.5, 0.1875)
    ent_source = with_ends(jax.random.randint(arg_keys[5], (ENTRIES,), 0, NB_ATM), jax.random.fold_in(arg_keys[5], 1), 0, NB_ATM - 1).astype(jnp.int32)
    ent_target_keys = jax.random.split(jax.random.fold_in(arg_keys[6], 1), ENTRIES // ENT_DEV)
    ent_target_turns = jax.random.permutation(jax.random.fold_in(arg_keys[6], 3), ENTRIES // ENT_DEV)
    ent_target = jax.vmap(lambda own, number: shared_out(jax.random.fold_in(arg_keys[6], 2), own, number, ENT_DEV, TILES, 1, CAP, 2))(ent_target_keys, ent_target_turns).reshape((ENTRIES, 1))
    ent_block = with_ends(jax.random.randint(arg_keys[7], (ENTRIES,), 0, NB_OCN), jax.random.fold_in(arg_keys[7], 1), 0, NB_OCN - 1).astype(jnp.int32)
    remap_weights = gaussian(arg_keys[8], (ENTRIES, BLK, BLK), BLK ** -0.5, 0.5, ((0, 32),))
    ocean_state = gaussian(arg_keys[9], (DO, OCELLS), 1.0, 6.0, ((1, 32),))
    land_sea = with_ends((jax.random.randint(arg_keys[10], (OCELLS,), 0, 10) < 7).astype(jnp.int32), jax.random.fold_in(arg_keys[10], 1), 0, 1)
    conv_kernel = gaussian(arg_keys[11], (DO, 9), 0.3, 2.5, (), jnp.float32)
    w_force = gaussian(arg_keys[12], (FX, DO), FX ** -0.5, 0.5)
    gain_ocn = jnp.clip(1.0 + 0.15 * jax.random.normal(arg_keys[13], (DO,), jnp.float32), 0.25, 1.75)
    w_up_ocn = gaussian(arg_keys[14], (DO, HO), DO ** -0.5, 0.4375)
    w_down_ocn = gaussian(arg_keys[15], (HO, DO), HO ** -0.5, 0.21875)
    return {"atm_state": atm_state, "gain_atm": gain_atm, "w_up_atm": w_up_atm, "w_down_atm": w_down_atm, "w_flux": w_flux, "ent_source": ent_source, "ent_target": ent_target, "ent_block": ent_block, "remap_weights": remap_weights, "ocean_state": ocean_state, "land_sea": land_sea, "conv_kernel": conv_kernel, "w_force": w_force, "gain_ocn": gain_ocn, "w_up_ocn": w_up_ocn, "w_down_ocn": w_down_ocn}


def atmosphere_layer(columns, gain_atm, w_up_atm, w_down_atm, w_flux):
    values = columns.astype(jnp.float32)
    centred = values - lax.optimization_barrier(jnp.mean(values, axis=-1, keepdims=True))
    spread_sq = lax.optimization_barrier(jnp.mean(centred * centred, axis=-1, keepdims=True))
    normed = (centred * lax.rsqrt(spread_sq + 1e-05) * gain_atm).astype(jnp.bfloat16)
    hidden = jax.nn.gelu(jnp.dot(normed, w_up_atm, preferred_element_type=jnp.float32)).astype(jnp.bfloat16)
    updated = (values + jnp.dot(hidden, w_down_atm, preferred_element_type=jnp.float32)).astype(jnp.bfloat16)
    surface = jnp.dot(updated, w_flux, preferred_element_type=jnp.float32).astype(jnp.bfloat16)
    return (updated, surface)

def column_mixing(padded, kernel, rows_out):
    summed = jnp.zeros((padded.shape[0], rows_out, padded.shape[2]), jnp.float32)
    for row_step in range(3):
        band_rows = padded[:, row_step:row_step + rows_out, :]
        for col_step in range(3):
            shifted = jnp.roll(band_rows, 1 - col_step, axis=2)
            summed = summed + kernel[:, 3 * row_step + col_step][:, None, None] * shifted
    return summed

def ocean_update(mixing, forcing, ocean_now, sea_mask, w_force, gain_ocn, w_up_ocn, w_down_ocn):
    contract = (((0,), (1,)), ((), ()))
    driven = mixing + lax.dot_general(w_force, forcing, contract, preferred_element_type=jnp.float32)
    centred = driven - lax.optimization_barrier(jnp.mean(driven, axis=0, keepdims=True))
    spread_sq = lax.optimization_barrier(jnp.mean(centred * centred, axis=0, keepdims=True))
    normed = (centred * lax.rsqrt(spread_sq + 1e-05) * gain_ocn[:, None]).astype(jnp.bfloat16)
    leading = (((0,), (0,)), ((), ()))
    hidden = jax.nn.gelu(lax.dot_general(w_up_ocn, normed, leading, preferred_element_type=jnp.float32)).astype(jnp.bfloat16)
    change = lax.dot_general(w_down_ocn, hidden, leading, preferred_element_type=jnp.float32)
    return (ocean_now.astype(jnp.float32) + sea_mask.astype(jnp.float32)[None, :] * change).astype(jnp.bfloat16)

def reference(atm_state, gain_atm, w_up_atm, w_down_atm, w_flux, ent_source, ent_target, ent_block, remap_weights, ocean_state, land_sea, conv_kernel, w_force, gain_ocn, w_up_ocn, w_down_ocn):
    devices = N_SEC * N_TILE
    atm_shards = atm_state.reshape(devices, C_ATM, DA)

    def one_block(columns):
        return atmosphere_layer(columns, gain_atm, w_up_atm, w_down_atm, w_flux)
    atm_next, surface = lax.map(one_block, atm_shards)
    atm_next = atm_next.reshape(devices * C_ATM, DA)
    surface_blocks = surface.reshape(devices * NB_ATM, BLK, FX)
    sources = ent_source.reshape(devices, ENT_DEV)
    targets = ent_target.reshape(devices, ENT_DEV)
    block_at = ent_block.reshape(devices, ENT_DEV)
    weights_all = remap_weights.reshape(devices, ENT_DEV, BLK, BLK)

    def accumulate(forcing, device):
        picked = surface_blocks[device * NB_ATM + sources[device]]
        weights = weights_all[device]
        remapped = jnp.einsum('eij,ejf->eif', weights.astype(jnp.float32), picked.astype(jnp.float32)).astype(jnp.bfloat16)
        remapped = lax.optimization_barrier(remapped)
        place_index = targets[device] * NB_OCN + block_at[device]
        return (forcing.at[place_index].add(remapped.astype(jnp.float32)), None)
    forcing, unused = lax.scan(accumulate, jnp.zeros((devices * NB_OCN, BLK, FX), jnp.float32), jnp.arange(devices, dtype=jnp.int32))
    forcing_half = forcing.astype(jnp.bfloat16).reshape(devices * OY * OX, FX)
    grid = ocean_state.astype(jnp.float32).reshape(DO, devices * OY, OX)
    padded = jnp.pad(grid, ((0, 0), (1, 1), (0, 0)))
    mixing = column_mixing(padded, conv_kernel, devices * OY).reshape(DO, devices * OY * OX)

    def ocean_block(device):
        first_cell = device * (OY * OX)
        return ocean_update(lax.dynamic_slice_in_dim(mixing, first_cell, OY * OX, 1), lax.dynamic_slice_in_dim(forcing_half, first_cell, OY * OX, 0), lax.dynamic_slice_in_dim(ocean_state, first_cell, OY * OX, 1), lax.dynamic_slice_in_dim(land_sea, first_cell, OY * OX, 0), w_force, gain_ocn, w_up_ocn, w_down_ocn)
    ocean_parts = lax.map(ocean_block, jnp.arange(devices, dtype=jnp.int32))
    ocean_next = jnp.moveaxis(ocean_parts, 0, 1).reshape(DO, devices * OY * OX)
    return (atm_next, ocean_next)
```

```python
import jax
import jax.numpy as jnp
from jax import lax
from jax.sharding import PartitionSpec as P

OX = 1440


def extended_2(block, sides, width):
    for axis, dim in sides:
        count = lax.axis_size(axis)
        forward = [(i, i + 1) for i in range(count - 1)]
        backward = [(target, source) for source, target in forward]
        low = lax.ppermute(
            lax.slice_in_dim(block, block.shape[dim] - width, None, axis=dim), axis, forward
        )
        high = lax.ppermute(lax.slice_in_dim(block, 0, width, axis=dim), axis, backward)
        block = jnp.concatenate([low, block, high], axis=dim)
    return block


def atmosphere_layer(columns, gain_atm, w_up_atm, w_down_atm, w_flux):
    values = columns.astype(jnp.float32)
    centred = values - jnp.mean(values, axis=-1, keepdims=True)
    spread_sq = jnp.mean(centred * centred, axis=-1, keepdims=True)
    normed = (centred * lax.rsqrt(spread_sq + 1e-05) * gain_atm).astype(jnp.bfloat16)
    hidden = jax.nn.gelu(jnp.dot(normed, w_up_atm, preferred_element_type=jnp.float32)).astype(
        jnp.bfloat16
    )
    updated = (values + jnp.dot(hidden, w_down_atm, preferred_element_type=jnp.float32)).astype(
        jnp.bfloat16
    )
    surface = jnp.dot(updated, w_flux, preferred_element_type=jnp.float32).astype(jnp.bfloat16)
    return (updated, surface)


def flat_mixing(padded_flat, kernel, row_len, cell_count):
    extended = jnp.pad(padded_flat.astype(jnp.float32), ((0, 0), (row_len, row_len)))
    column_at = (jnp.arange(cell_count, dtype=jnp.int32) % row_len)[None, :]
    first_col = column_at == 0
    last_col = column_at == row_len - 1

    def window(offset):
        return lax.slice_in_dim(extended, row_len + offset, row_len + offset + cell_count, axis=1)

    summed = jnp.zeros((padded_flat.shape[0], cell_count), jnp.float32)
    for row_step in range(3):
        base = row_step * row_len
        for col_step in range(3):
            if col_step == 0:
                shifted = jnp.where(first_col, window(base + row_len - 1), window(base - 1))
            elif col_step == 2:
                shifted = jnp.where(last_col, window(base - row_len + 1), window(base + 1))
            else:
                shifted = window(base)
            summed = summed + kernel[:, 3 * row_step + col_step][:, None] * shifted
    return summed


def ocean_update(mixing, forcing, ocean_now, sea_mask, w_force, gain_ocn, w_up_ocn, w_down_ocn):
    contract = (((0,), (1,)), ((), ()))
    driven = mixing + lax.dot_general(
        w_force, forcing, contract, preferred_element_type=jnp.float32
    )
    centred = driven - jnp.mean(driven, axis=0, keepdims=True)
    spread_sq = jnp.mean(centred * centred, axis=0, keepdims=True)
    normed = (centred * lax.rsqrt(spread_sq + 1e-05) * gain_ocn[:, None]).astype(jnp.bfloat16)
    leading = (((0,), (0,)), ((), ()))
    hidden = jax.nn.gelu(
        lax.dot_general(w_up_ocn, normed, leading, preferred_element_type=jnp.float32)
    ).astype(jnp.bfloat16)
    change = lax.dot_general(w_down_ocn, hidden, leading, preferred_element_type=jnp.float32)
    return (ocean_now.astype(jnp.float32) + sea_mask.astype(jnp.float32)[None, :] * change).astype(
        jnp.bfloat16
    )


def local(
    atm_state,
    gain_atm,
    w_up_atm,
    w_down_atm,
    w_flux,
    ent_source,
    ent_target,
    ent_block,
    remap_weights,
    ocean_state,
    land_sea,
    conv_kernel,
    w_force,
    gain_ocn,
    w_up_ocn,
    w_down_ocn,
):
    cell_count = ocean_state.shape[1]
    padded = extended_2(ocean_state, ((("sec", "tile"), 1),), OX)
    mixing = flat_mixing(padded, conv_kernel, OX, cell_count)
    atm_next, surface = atmosphere_layer(atm_state, gain_atm, w_up_atm, w_down_atm, w_flux)
    block_rows = remap_weights.shape[1]
    features = surface.shape[1]
    atm_blocks = surface.shape[0] // block_rows
    surface_flat = surface.reshape(atm_blocks, block_rows * features)
    sections = lax.axis_size("sec")
    devices = sections * lax.axis_size("tile")
    entries = ent_source.shape[0]
    capacity = max(2, 2 * entries // devices)
    targets = ent_target[:, 0]
    matches = (targets[:, None] == jnp.arange(devices, dtype=jnp.int32)[None, :]).astype(jnp.int32)
    before = (
        jnp.arange(entries, dtype=jnp.int32)[:, None] > jnp.arange(entries, dtype=jnp.int32)[None, :]
    ).astype(jnp.bfloat16)
    earlier = jnp.dot(
        before, matches.astype(jnp.bfloat16), preferred_element_type=jnp.float32
    ).astype(jnp.int32)
    position = jnp.sum(earlier * matches, axis=1)
    slot_index = targets * capacity + position
    source_pick = (ent_source[:, None] == jnp.arange(atm_blocks, dtype=jnp.int32)[None, :]).astype(
        jnp.bfloat16
    )
    picked = (
        jnp.dot(source_pick, surface_flat, preferred_element_type=jnp.float32)
        .astype(jnp.bfloat16)
        .reshape(entries, block_rows, features)
    )
    payload = jnp.einsum(
        "eij,ejf->eif", remap_weights, picked, preferred_element_type=jnp.float32
    ).astype(jnp.bfloat16)
    item_shape = payload.shape[1:]
    slot_count = devices * capacity
    slot_table_int = (
        jnp.arange(slot_count, dtype=jnp.int32)[:, None] == slot_index[None, :]
    ).astype(jnp.int32)
    slot_table = slot_table_int.astype(jnp.bfloat16)
    outgoing = (
        jnp.dot(slot_table, payload.reshape(entries, -1), preferred_element_type=jnp.float32)
        .astype(jnp.bfloat16)
        .reshape((slot_count,) + item_shape)
    )
    labels = jnp.sum(slot_table_int * (ent_block[None, :] + 1), axis=1) - 1
    arrived, arrived_labels = (
        lax.all_to_all(
            outgoing.reshape((devices, capacity) + item_shape),
            ("sec", "tile"),
            split_axis=0,
            concat_axis=0,
            tiled=True,
        ),
        lax.all_to_all(
            labels.reshape(devices, capacity),
            ("sec", "tile"),
            split_axis=0,
            concat_axis=0,
            tiled=True,
        ),
    )
    arrived = arrived.reshape((slot_count,) + item_shape)
    arrived_labels = arrived_labels.reshape(slot_count)
    ocean_blocks = cell_count // block_rows
    select = (jnp.arange(ocean_blocks, dtype=jnp.int32)[:, None] == arrived_labels[None, :]).astype(
        jnp.bfloat16
    )
    forcing = (
        jnp.einsum("ks,sif->kif", select, arrived, preferred_element_type=jnp.float32)
        .astype(jnp.bfloat16)
        .reshape(cell_count, features)
    )
    ocean_next = ocean_update(
        mixing, forcing, ocean_state, land_sea, w_force, gain_ocn, w_up_ocn, w_down_ocn
    )
    return (atm_next, ocean_next)


def solution(mesh):
    placed = (
        P(("sec", "tile"), None),
        P(),
        P(),
        P(),
        P(),
        P(("sec", "tile")),
        P(("sec", "tile"), None),
        P(("sec", "tile")),
        P(("sec", "tile"), None, None),
        P(None, ("sec", "tile")),
        P(("sec", "tile")),
        P(),
        P(),
        P(),
        P(),
        P(),
    )
    return jax.shard_map(
        local,
        mesh=mesh,
        in_specs=placed,
        out_specs=(P(("sec", "tile"), None), P(None, ("sec", "tile"))),
        check_vma=False,
    )
```

```python
import functools
import math

import jax
import jax.numpy as jnp
from jax import lax
from jax.experimental import pallas as pl
from jax.experimental.pallas import tpu as pltpu
from jax.sharding import Mesh, PartitionSpec as P

OX = 1440
ALL = ("sec", "half", "near")
PEERS = ("sec", "near")
F32 = jnp.float32
BF16 = jnp.bfloat16


def gelu(x):
    half = 0.5 * x
    return half + half * jnp.tanh(x * (0.7978845608028654 + 0.035677408136300125 * (x * x)))


def normalised(values, axis):
    centred = values - jnp.mean(values, axis=axis, keepdims=True)
    spread_sq = jnp.mean(centred * centred, axis=axis, keepdims=True)
    return centred * lax.rsqrt(spread_sq + 1e-05)


def whole(shape):
    return pl.BlockSpec(shape, lambda *_: (0,) * len(shape))


def atm_kernel(x_ref, gain_ref, up_ref, down_ref, flux_ref, next_ref, surface_ref, normed, total):
    step = pl.program_id(0)

    @pl.when(step == 0)
    def _():
        values = x_ref[...].astype(F32)
        normed[...] = (normalised(values, -1) * gain_ref[...]).astype(BF16)
        total[...] = values

    hidden = gelu(jnp.dot(normed[...], up_ref[...], preferred_element_type=F32)).astype(BF16)
    total[...] += jnp.dot(hidden, down_ref[...], preferred_element_type=F32)

    @pl.when(step == pl.num_programs(0) - 1)
    def _():
        updated = total[...].astype(BF16)
        next_ref[...] = updated
        surface_ref[...] = jnp.dot(updated, flux_ref[...], preferred_element_type=F32).astype(BF16)


def atmosphere(columns, gain, w_up, w_down, w_flux):
    rows, width = columns.shape
    hidden = w_up.shape[1]
    part = hidden // 4
    return pl.pallas_call(
        atm_kernel,
        name="atmosphere",
        grid=(hidden // part,),
        in_specs=[
            whole((rows, width)),
            whole((1, width)),
            pl.BlockSpec((width, part), lambda i: (0, i)),
            pl.BlockSpec((part, width), lambda i: (i, 0)),
            whole(w_flux.shape),
        ],
        out_specs=[whole((rows, width)), whole((rows, w_flux.shape[1]))],
        out_shape=[
            jax.ShapeDtypeStruct((rows, width), BF16),
            jax.ShapeDtypeStruct((rows, w_flux.shape[1]), BF16),
        ],
        scratch_shapes=[pltpu.VMEM((rows, width), BF16), pltpu.VMEM((rows, width), F32)],
        compiler_params=pltpu.CompilerParams(vmem_limit_bytes=48 << 20),
    )(columns, gain[None, :], w_up, w_down, w_flux)


def remap_kernel(first, group, slot_ref, source_ref, surface_ref, weight_ref, out_ref, made, sems):
    step = pl.program_id(0)
    slots = out_ref.shape[0]
    entries = made.shape[0]

    def copy(entry):
        slot = slot_ref[entry] - first
        return pltpu.make_async_copy(made.at[entry], out_ref.at[slot], sems.at[entry])

    def mine(entry):
        slot = slot_ref[entry] - first
        return (slot >= 0) & (slot < slots)

    for i in range(group):
        entry = step * group + i

        @pl.when(mine(entry))
        def _():
            made[entry] = jnp.dot(
                weight_ref[i], surface_ref[source_ref[entry]], preferred_element_type=F32
            ).astype(BF16)
            copy(entry).start()

    @pl.when(step == pl.num_programs(0) - 1)
    def _():
        def drain(entry, carry):
            @pl.when(mine(entry))
            def _():
                copy(entry).wait()

            return carry

        lax.fori_loop(0, entries, drain, 0)


def remapped(first, slots, slot_of, source, surface, weights):
    entries, block, _ = weights.shape
    group = 16 if entries % 16 == 0 else 1
    return pl.pallas_call(
        functools.partial(remap_kernel, first, group),
        name="remap",
        grid_spec=pltpu.PrefetchScalarGridSpec(
            num_scalar_prefetch=2,
            grid=(entries // group,),
            in_specs=[
                whole(surface.shape),
                pl.BlockSpec((group, block, block), lambda i, *_: (i, 0, 0)),
            ],
            out_specs=pl.BlockSpec(memory_space=pltpu.HBM),
            scratch_shapes=[
                pltpu.VMEM((entries, block, surface.shape[2]), BF16),
                pltpu.SemaphoreType.DMA((entries,)),
            ],
        ),
        out_shape=pltpu.HBM((slots, block, surface.shape[2]), BF16),
        compiler_params=pltpu.CompilerParams(vmem_limit_bytes=32 << 20),
    )(slot_of, source, surface, weights)


def merge_kernel(group, label_ref, arrived_ref, out_ref, total):
    step = pl.program_id(0)

    @pl.when(step == 0)
    def _():
        total[...] = jnp.zeros_like(total)

    for i in range(group):
        label = label_ref[step * group + i]

        @pl.when(label >= 0)
        def _():
            total[label] += arrived_ref[i].astype(F32)

    @pl.when(step == pl.num_programs(0) - 1)
    def _():
        out_ref[...] = total[...].astype(BF16)


def merged(labels, arrived, blocks):
    slots, block, features = arrived.shape
    group = 16 if slots % 16 == 0 else 1
    return pl.pallas_call(
        functools.partial(merge_kernel, group),
        name="merge",
        grid_spec=pltpu.PrefetchScalarGridSpec(
            num_scalar_prefetch=1,
            grid=(slots // group,),
            in_specs=[pl.BlockSpec((group, block, features), lambda i, *_: (i, 0, 0))],
            out_specs=whole((blocks, block, features)),
            scratch_shapes=[pltpu.VMEM((blocks, block, features), F32)],
        ),
        out_shape=jax.ShapeDtypeStruct((blocks, block, features), BF16),
        compiler_params=pltpu.CompilerParams(vmem_limit_bytes=32 << 20),
    )(labels, arrived)


def ocean_kernel(mix_ref, near_ref, far_ref, now_ref, sea_ref, force_ref, gain_ref, up_ref, down_ref, out_ref):
    forcing = (near_ref[...].astype(F32) + far_ref[...].astype(F32)).astype(BF16)
    driven = mix_ref[...] + lax.dot_general(
        force_ref[...], forcing, (((1,), (1,)), ((), ())), preferred_element_type=F32
    )
    normed = (normalised(driven, 0) * gain_ref[...]).astype(BF16)
    hidden = gelu(jnp.dot(up_ref[...], normed, preferred_element_type=F32)).astype(BF16)
    change = jnp.dot(down_ref[...], hidden, preferred_element_type=F32)
    out_ref[...] = (
        now_ref[...].astype(F32) + sea_ref[...].astype(F32) * change
    ).astype(BF16)


def ocean(mixing, near, far, now, sea, w_force, gain, w_up, w_down):
    channels, cells = now.shape
    features = near.shape[1]
    part = cells // 5
    if part % 128:
        part = cells
    tall = pl.BlockSpec((channels, part), lambda i: (0, i))
    flat = pl.BlockSpec((part, features), lambda i: (i, 0))
    return pl.pallas_call(
        ocean_kernel,
        name="ocean",
        grid=(cells // part,),
        in_specs=[
            tall,
            flat,
            flat,
            tall,
            pl.BlockSpec((1, part), lambda i: (0, i)),
            whole(w_force.shape),
            whole((channels, 1)),
            whole(w_up.shape),
            whole(w_down.shape),
        ],
        out_specs=tall,
        out_shape=jax.ShapeDtypeStruct((channels, cells), BF16),
        compiler_params=pltpu.CompilerParams(vmem_limit_bytes=48 << 20),
    )(mixing, near, far, now, sea[None, :], w_force, gain[:, None], w_up, w_down)


def edge_rows(block):
    count = math.prod(lax.axis_size(axis) for axis in ALL)
    forward = [(i, i + 1) for i in range(count - 1)]
    backward = [(target, source) for source, target in forward]
    low = lax.ppermute(block[:, -OX:], ALL, forward)
    high = lax.ppermute(block[:, :OX], ALL, backward)
    return low, high


def flat_mixing(padded_flat, kernel, row_len, cell_count):
    extended = jnp.pad(padded_flat.astype(F32), ((0, 0), (row_len, row_len)))
    column_at = (jnp.arange(cell_count, dtype=jnp.int32) % row_len)[None, :]
    first_col = column_at == 0
    last_col = column_at == row_len - 1

    def window(offset):
        return lax.slice_in_dim(extended, row_len + offset, row_len + offset + cell_count, axis=1)

    summed = jnp.zeros((padded_flat.shape[0], cell_count), F32)
    for row_step in range(3):
        base = row_step * row_len
        for col_step in range(3):
            if col_step == 0:
                shifted = jnp.where(first_col, window(base + row_len - 1), window(base - 1))
            elif col_step == 2:
                shifted = jnp.where(last_col, window(base - row_len + 1), window(base + 1))
            else:
                shifted = window(base)
            summed = summed + kernel[:, 3 * row_step + col_step][:, None] * shifted
    return summed


def local(
    atm_state,
    gain_atm,
    w_up_atm,
    w_down_atm,
    w_flux,
    ent_source,
    ent_target,
    ent_block,
    remap_weights,
    ocean_state,
    land_sea,
    conv_kernel,
    w_force,
    gain_ocn,
    w_up_ocn,
    w_down_ocn,
):
    sections, halves, nears = (lax.axis_size(axis) for axis in ALL)
    sec, half, near = (lax.axis_index(axis) for axis in ALL)
    peers = sections * nears
    entries, block_rows, _ = remap_weights.shape
    capacity = max(2, 2 * entries // (peers * halves))
    slots = peers * capacity
    cell_count = ocean_state.shape[1]
    ocean_blocks = cell_count // block_rows
    low, high = edge_rows(ocean_state)

    targets = ent_target[:, 0]
    at = jnp.arange(entries, dtype=jnp.int32)
    rank = jnp.sum(
        ((targets[:, None] == targets[None, :]) & (at[:, None] > at[None, :])).astype(jnp.int32),
        axis=1,
    )
    peer = targets // (halves * nears) * nears + targets % nears
    far = targets // nears % halves != half
    slot_of = peer * capacity + rank + jnp.where(far, 0, slots)

    place = jnp.arange(2 * slots, dtype=jnp.int32)
    sent_labels = (
        jnp.sum(jnp.where(place[:, None] == slot_of[None, :], ent_block[None, :] + 1, 0), axis=1)
        - 1
    )
    sent_labels = sent_labels.reshape(2, peers, capacity).transpose(1, 0, 2)
    got_labels = lax.all_to_all(
        sent_labels.reshape(peers, 2 * capacity), PEERS, split_axis=0, concat_axis=0, tiled=True
    ).reshape(peers, 2, capacity)
    far_labels = got_labels[:, 0].reshape(slots)
    near_labels = got_labels[:, 1].reshape(slots)

    atm_next, surface = atmosphere(atm_state, gain_atm, w_up_atm, w_down_atm, w_flux)
    surface = surface.reshape(-1, block_rows, surface.shape[1])
    surface, low, high, far_labels, near_labels = lax.optimization_barrier(
        (surface, low, high, far_labels, near_labels)
    )

    def exchange(values):
        return lax.all_to_all(values, PEERS, split_axis=0, concat_axis=0, tiled=True)

    far_arrived = exchange(remapped(0, slots, slot_of, ent_source, surface, remap_weights))
    near_made = remapped(slots, slots, slot_of, ent_source, surface, remap_weights)
    padded = jnp.concatenate([low, ocean_state, high], axis=1)
    mixing = flat_mixing(padded, conv_kernel, OX, cell_count)
    far_arrived, near_made, mixing = lax.optimization_barrier((far_arrived, near_made, mixing))
    near_arrived = exchange(near_made)
    far_sum = merged(far_labels, far_arrived, ocean_blocks)
    far_sum = lax.ppermute(far_sum, "half", [(0, 1), (1, 0)])
    near_sum = merged(near_labels, near_arrived, ocean_blocks)
    features = far_sum.shape[2]
    ocean_next = ocean(
        mixing,
        near_sum.reshape(cell_count, features),
        far_sum.reshape(cell_count, features),
        ocean_state,
        land_sea,
        w_force.T,
        gain_ocn,
        w_up_ocn.T,
        w_down_ocn.T,
    )
    return (atm_next, ocean_next)


def solution(mesh):
    sections, tiles = mesh.shape["sec"], mesh.shape["tile"]
    fine = Mesh(mesh.devices.reshape(sections, 2, tiles // 2), ALL)
    placed = (
        P(ALL, None),
        P(),
        P(),
        P(),
        P(),
        P(ALL),
        P(ALL, None),
        P(ALL),
        P(ALL, None, None),
        P(None, ALL),
        P(ALL),
        P(),
        P(),
        P(),
        P(),
        P(),
    )
    return jax.shard_map(
        local,
        mesh=fine,
        in_specs=placed,
        out_specs=(P(ALL, None), P(None, ALL)),
        check_vma=False,
    )
```

```python
import functools
import math

import jax
import jax.numpy as jnp
from jax import lax
from jax.experimental import pallas as pl
from jax.experimental.pallas import tpu as pltpu
from jax.sharding import Mesh, PartitionSpec as P

OX = 1440
ALL = ("sec", "half", "near")
PEERS = ("sec", "near")
F32 = jnp.float32
BF16 = jnp.bfloat16


def gelu(x):
    half = 0.5 * x
    return half + half * jnp.tanh(x * (0.7978845608028654 + 0.035677408136300125 * (x * x)))


def normalised(values, axis):
    centred = values - jnp.mean(values, axis=axis, keepdims=True)
    spread_sq = jnp.mean(centred * centred, axis=axis, keepdims=True)
    return centred * lax.rsqrt(spread_sq + 1e-05)


def in_hbm(value):
    return pltpu.with_memory_space_constraint(value, pltpu.HBM)


def whole(shape):
    return pl.BlockSpec(shape, lambda *_: (0,) * len(shape))


def split(index, size):
    if size & (size - 1) == 0:
        return index >> (size.bit_length() - 1), index & (size - 1)
    return lax.div(index, size), lax.rem(index, size)


def pick(plan, want_far, half_ref, target_ref, listed, slots, counts):
    _, halves, nears, capacity = plan

    def none(tile, carry):
        counts[tile] = 0
        return carry

    def step(entry, count):
        target = target_ref[entry]
        rank = counts[target]
        counts[target] = rank + 1
        upper, near = split(target, nears)
        sec, half = split(upper, halves)
        listed[count] = entry
        slots[count] = (sec * nears + near) * capacity + rank
        far = (half != half_ref[0]).astype(jnp.int32)
        return count + (far if want_far else 1 - far)

    lax.fori_loop(0, counts.shape[0], none, 0)
    return lax.fori_loop(0, target_ref.shape[0], step, jnp.int32(0), unroll=4)


def multiply(plan, count, source_ref, block_ref, surface_ref, weights, listed, slots, made, labels, tile, out_ref, sems, tile_sem):
    capacity = plan[3]
    block = weights.shape[1]
    labels[...] = jnp.full_like(labels, -1)
    lane = lax.broadcasted_iota(jnp.int32, (1, labels.shape[1]), 1)

    def copy(at):
        peer, rank = split(slots[at], capacity)
        rows = pl.ds(pl.multiple_of(rank * block, block), block)
        return pltpu.make_async_copy(made.at[at], out_ref.at[peer, rows], sems.at[at])

    def group(size, first):
        for i in range(size):
            entry = listed[first + i]
            rows = pl.ds(pl.multiple_of(source_ref[entry] * block, block), block)
            made[first + i] = jnp.dot(
                weights[entry], surface_ref[rows, :], preferred_element_type=F32
            ).astype(BF16)
            peer, rank = split(slots[first + i], capacity)
            row = labels[pl.ds(peer, 1), :]
            labels[pl.ds(peer, 1), :] = jnp.where(lane == rank, block_ref[entry], row)
        for i in range(size):
            copy(first + i).start()

    def eight(i, carry):
        group(8, i * 8)
        return carry

    def one(i, carry):
        group(1, i)
        return carry

    def drain(i, carry):
        copy(i).wait()
        return carry

    full = count >> 3
    lax.fori_loop(0, full, eight, 0)
    lax.fori_loop(full * 8, count, one, 0)
    tile[...] = jnp.broadcast_to(labels[...].astype(F32)[:, None, :], tile.shape).astype(BF16)
    told = pltpu.make_async_copy(
        tile, out_ref.at[:, pl.ds(capacity * block, tile.shape[1])], tile_sem
    )
    told.start()
    lax.fori_loop(0, count, drain, 0)
    told.wait()


def remap_scratch(plan, entries, block, features):
    sections, halves, nears, _ = plan
    peers = sections * nears
    return [
        pltpu.SMEM((entries + 1,), jnp.int32),
        pltpu.SMEM((entries + 1,), jnp.int32),
        pltpu.SMEM((sections * halves * nears,), jnp.int32),
        pltpu.VMEM((entries, block, block), BF16),
        pltpu.VMEM((entries, block, features), BF16),
        pltpu.VMEM((peers, 128), jnp.int32),
        pltpu.VMEM((peers, 16, features), BF16),
        pltpu.SemaphoreType.DMA((entries,)),
        pltpu.SemaphoreType.DMA,
        pltpu.SemaphoreType.DMA,
    ]


def atm_kernel(
    plan,
    half_ref,
    target_ref,
    source_ref,
    block_ref,
    x_ref,
    gain_ref,
    up_ref,
    down_ref,
    flux_ref,
    weight_ref,
    next_ref,
    surface_ref,
    far_ref,
    normed,
    total,
    listed,
    slots,
    counts,
    weights,
    made,
    labels,
    tile,
    sems,
    tile_sem,
    weight_sem,
):
    step = pl.program_id(0)
    last = step == pl.num_programs(0) - 1
    parts = [slice(at, at + x_ref.shape[0] // 2) for at in (0, x_ref.shape[0] // 2)]
    fetch = pltpu.make_async_copy(weight_ref, weights, weight_sem)

    @pl.when(step == 0)
    def _():
        for rows in parts:
            values = x_ref[rows, :].astype(F32)
            normed[rows, :] = (normalised(values, -1) * gain_ref[...]).astype(BF16)
            total[rows, :] = values

    @pl.when(step == 1)
    def _():
        fetch.start()

    for rows in parts:
        raised = jnp.dot(normed[rows, :], up_ref[...], preferred_element_type=F32)
        hidden = gelu(raised.astype(BF16))
        total[rows, :] += jnp.dot(hidden, down_ref[...], preferred_element_type=F32)

    @pl.when(last)
    def _():
        for rows in parts:
            updated = total[rows, :].astype(BF16)
            next_ref[rows, :] = updated
            surface_ref[rows, :] = jnp.dot(
                updated, flux_ref[...], preferred_element_type=F32
            ).astype(BF16)
        count = pick(plan, True, half_ref, target_ref, listed, slots, counts)
        fetch.wait()
        multiply(plan, count, source_ref, block_ref, surface_ref, weights, listed, slots, made, labels, tile, far_ref, sems, tile_sem)


def atmosphere(plan, half, target, source, target_block, columns, gain, w_up, w_down, w_flux, weights):
    rows, width = columns.shape
    features = w_flux.shape[1]
    inner = w_up.shape[1]
    entries, block, _ = weights.shape
    part = inner // 4
    peers = plan[0] * plan[2]
    return pl.pallas_call(
        functools.partial(atm_kernel, plan),
        name="atmosphere",
        grid_spec=pltpu.PrefetchScalarGridSpec(
            num_scalar_prefetch=4,
            grid=(inner // part,),
            in_specs=[
                whole((rows, width)),
                whole((1, width)),
                pl.BlockSpec((width, part), lambda i, *_: (0, i)),
                pl.BlockSpec((part, width), lambda i, *_: (i, 0)),
                whole(w_flux.shape),
                pl.BlockSpec(memory_space=pltpu.HBM),
            ],
            out_specs=[
                whole((rows, width)),
                whole((rows, features)),
                pl.BlockSpec(memory_space=pltpu.HBM),
            ],
            scratch_shapes=[
                pltpu.VMEM((rows, width), BF16),
                pltpu.VMEM((rows, width), F32),
                *remap_scratch(plan, entries, block, features),
            ],
        ),
        out_shape=[
            pltpu.HBM((rows, width), BF16),
            pltpu.HBM((rows, features), BF16),
            pltpu.HBM((peers, plan[3] * block + 16, features), BF16),
        ],
        compiler_params=pltpu.CompilerParams(vmem_limit_bytes=56 << 20),
    )(
        half,
        target,
        source,
        target_block,
        in_hbm(columns),
        in_hbm(gain[None, :]),
        in_hbm(w_up),
        in_hbm(w_down),
        in_hbm(w_flux),
        in_hbm(weights),
    )


def near_kernel(
    plan,
    half_ref,
    target_ref,
    source_ref,
    block_ref,
    surface_ref,
    weight_ref,
    near_ref,
    listed,
    slots,
    counts,
    weights,
    made,
    labels,
    tile,
    sems,
    tile_sem,
    weight_sem,
):
    fetch = pltpu.make_async_copy(weight_ref, weights, weight_sem)
    fetch.start()
    count = pick(plan, False, half_ref, target_ref, listed, slots, counts)
    fetch.wait()
    multiply(plan, count, source_ref, block_ref, surface_ref, weights, listed, slots, made, labels, tile, near_ref, sems, tile_sem)


def near_remap(plan, half, target, source, target_block, surface, weights):
    entries, block, _ = weights.shape
    features = surface.shape[1]
    peers = plan[0] * plan[2]
    return pl.pallas_call(
        functools.partial(near_kernel, plan),
        name="near_remap",
        grid_spec=pltpu.PrefetchScalarGridSpec(
            num_scalar_prefetch=4,
            grid=(1,),
            in_specs=[whole(surface.shape), pl.BlockSpec(memory_space=pltpu.HBM)],
            out_specs=pl.BlockSpec(memory_space=pltpu.HBM),
            scratch_shapes=remap_scratch(plan, entries, block, features),
        ),
        out_shape=pltpu.HBM((peers, plan[3] * block + 16, features), BF16),
        compiler_params=pltpu.CompilerParams(vmem_limit_bytes=48 << 20),
    )(half, target, source, target_block, in_hbm(surface), in_hbm(weights))


def merge_kernel(capacity, arrived_ref, out_ref, arrived, tile, listed, labels, total, sems, tile_sem):
    peers = arrived.shape[0]
    block = out_ref.shape[1]

    def fetch(peer):
        return pltpu.make_async_copy(
            arrived_ref.at[peer, pl.ds(0, capacity * block)], arrived.at[peer], sems.at[peer]
        )

    told = pltpu.make_async_copy(
        arrived_ref.at[:, pl.ds(capacity * block, tile.shape[1])], tile, tile_sem
    )
    told.start()
    for peer in range(peers):
        fetch(peer).start()
    total[...] = jnp.zeros_like(total)
    told.wait()
    listed[...] = jnp.max(tile[...].astype(F32), axis=1).astype(jnp.int32)
    read = pltpu.make_async_copy(listed, labels, tile_sem)
    read.start()
    read.wait()

    def add(peer, carry):
        fetch(peer).wait()
        for rank in range(capacity):
            label = labels[peer, rank]

            @pl.when(label >= 0)
            def _():
                total[label] += arrived[peer, rank * block : (rank + 1) * block].astype(F32)

        return carry

    lax.fori_loop(0, peers, add, 0)
    out_ref[...] = total[...].astype(BF16)


def merged(capacity, arrived, blocks, block):
    peers, _, features = arrived.shape
    return pl.pallas_call(
        functools.partial(merge_kernel, capacity),
        name="merge",
        grid=(1,),
        in_specs=[pl.BlockSpec(memory_space=pltpu.HBM)],
        out_specs=whole((blocks, block, features)),
        scratch_shapes=[
            pltpu.VMEM((peers, capacity * block, features), BF16),
            pltpu.VMEM((peers, 16, features), BF16),
            pltpu.VMEM((peers, features), jnp.int32),
            pltpu.SMEM((peers, features), jnp.int32),
            pltpu.VMEM((blocks, block, features), F32),
            pltpu.SemaphoreType.DMA((peers,)),
            pltpu.SemaphoreType.DMA,
        ],
        out_shape=pltpu.HBM((blocks, block, features), BF16),
        compiler_params=pltpu.CompilerParams(vmem_limit_bytes=32 << 20),
    )(in_hbm(arrived))


def ocean_kernel(mix_ref, near_ref, far_ref, now_ref, sea_ref, force_ref, gain_ref, up_ref, down_ref, out_ref):
    forcing = (near_ref[...].astype(F32) + far_ref[...].astype(F32)).astype(BF16)
    driven = mix_ref[...] + lax.dot_general(
        force_ref[...], forcing, (((1,), (1,)), ((), ())), preferred_element_type=F32
    )
    normed = (normalised(driven, 0) * gain_ref[...]).astype(BF16)
    hidden = gelu(jnp.dot(up_ref[...], normed, preferred_element_type=F32)).astype(BF16)
    change = jnp.dot(down_ref[...], hidden, preferred_element_type=F32)
    out_ref[...] = (
        now_ref[...].astype(F32) + sea_ref[...].astype(F32) * change
    ).astype(BF16)


def ocean(mixing, near, far, now, sea, w_force, gain, w_up, w_down):
    channels, cells = now.shape
    features = near.shape[1]
    part = cells // 5
    if part % 128:
        part = cells
    tall = pl.BlockSpec((channels, part), lambda i: (0, i))
    flat = pl.BlockSpec((part, features), lambda i: (i, 0))
    return pl.pallas_call(
        ocean_kernel,
        name="ocean",
        grid=(cells // part,),
        in_specs=[
            tall,
            flat,
            flat,
            tall,
            pl.BlockSpec((1, part), lambda i: (0, i)),
            whole(w_force.shape),
            whole((channels, 1)),
            whole(w_up.shape),
            whole(w_down.shape),
        ],
        out_specs=tall,
        out_shape=jax.ShapeDtypeStruct((channels, cells), BF16),
        compiler_params=pltpu.CompilerParams(vmem_limit_bytes=48 << 20),
    )(
        in_hbm(mixing),
        in_hbm(near),
        far,
        in_hbm(now),
        sea[None, :],
        w_force,
        gain[:, None],
        w_up,
        w_down,
    )


def edge_rows(block):
    count = math.prod(lax.axis_size(axis) for axis in ALL)
    forward = [(i, i + 1) for i in range(count - 1)]
    backward = [(target, source) for source, target in forward]
    low = lax.ppermute(block[:, -OX:], ALL, forward)
    high = lax.ppermute(block[:, :OX], ALL, backward)
    return low, high


def flat_mixing(padded_flat, kernel, row_len, cell_count):
    extended = jnp.pad(padded_flat.astype(F32), ((0, 0), (row_len, row_len)))
    column_at = (jnp.arange(cell_count, dtype=jnp.int32) % row_len)[None, :]
    first_col = column_at == 0
    last_col = column_at == row_len - 1

    def window(offset):
        return lax.slice_in_dim(extended, row_len + offset, row_len + offset + cell_count, axis=1)

    summed = jnp.zeros((padded_flat.shape[0], cell_count), F32)
    for row_step in range(3):
        base = row_step * row_len
        for col_step in range(3):
            if col_step == 0:
                shifted = jnp.where(first_col, window(base + row_len - 1), window(base - 1))
            elif col_step == 2:
                shifted = jnp.where(last_col, window(base - row_len + 1), window(base + 1))
            else:
                shifted = window(base)
            summed = summed + kernel[:, 3 * row_step + col_step][:, None] * shifted
    return summed


def local(
    atm_state,
    gain_atm,
    w_up_atm,
    w_down_atm,
    w_flux,
    ent_source,
    ent_target,
    ent_block,
    remap_weights,
    ocean_state,
    land_sea,
    conv_kernel,
    w_force,
    gain_ocn,
    w_up_ocn,
    w_down_ocn,
):
    sections, halves, nears = (lax.axis_size(axis) for axis in ALL)
    half = lax.axis_index("half")
    peers = sections * nears
    entries, block_rows, _ = remap_weights.shape
    capacity = max(2, 2 * entries // (peers * halves))
    cell_count = ocean_state.shape[1]
    ocean_blocks = cell_count // block_rows

    def exchange(values):
        return lax.all_to_all(values, PEERS, split_axis=0, concat_axis=0, tiled=True)

    plan = (sections, halves, nears, capacity)
    entry = (half[None], ent_target[:, 0], ent_source, ent_block)
    atm_next, surface, far_made = atmosphere(
        plan, *entry, atm_state, gain_atm, w_up_atm, w_down_atm, w_flux, remap_weights
    )
    far_made, edge_source = lax.optimization_barrier((far_made, ocean_state))
    far_arrived = exchange(far_made)
    near_made = near_remap(plan, *entry, surface, remap_weights)
    low, high = edge_rows(edge_source)
    padded = jnp.concatenate([low, ocean_state, high], axis=1)
    mixing = flat_mixing(padded, conv_kernel, OX, cell_count)
    far_arrived, near_made, mixing = lax.optimization_barrier((far_arrived, near_made, mixing))
    near_arrived = exchange(near_made)
    far_sum = merged(capacity, far_arrived, ocean_blocks, block_rows)
    far_sum = lax.ppermute(far_sum, "half", [(0, 1), (1, 0)])
    near_sum = merged(capacity, near_arrived, ocean_blocks, block_rows)
    features = far_sum.shape[2]
    ocean_next = ocean(
        mixing,
        near_sum.reshape(cell_count, features),
        far_sum.reshape(cell_count, features),
        ocean_state,
        land_sea,
        w_force.T,
        gain_ocn,
        w_up_ocn.T,
        w_down_ocn.T,
    )
    return (atm_next, ocean_next)


def solution(mesh):
    sections, tiles = mesh.shape["sec"], mesh.shape["tile"]
    fine = Mesh(mesh.devices.reshape(sections, 2, tiles // 2), ALL)
    placed = (
        P(ALL, None),
        P(),
        P(),
        P(),
        P(),
        P(ALL),
        P(ALL, None),
        P(ALL),
        P(ALL, None, None),
        P(None, ALL),
        P(ALL),
        P(),
        P(),
        P(),
        P(),
        P(),
    )
    return jax.shard_map(
        local,
        mesh=fine,
        in_specs=placed,
        out_specs=(P(ALL, None), P(None, ALL)),
        check_vma=False,
    )
```

```python
import functools
import math

import jax
import jax.numpy as jnp
from jax import lax
from jax.experimental import pallas as pl
from jax.experimental.pallas import tpu as pltpu
from jax.sharding import Mesh, PartitionSpec as P

OX = 1440
ALL = ("sec", "half", "near")
PEERS = ("sec", "near")
F32 = jnp.float32
BF16 = jnp.bfloat16


def gelu(x):
    half = 0.5 * x
    return half + half * jnp.tanh(x * (0.7978845608028654 + 0.035677408136300125 * (x * x)))


def normalised(values, axis):
    centred = values - jnp.mean(values, axis=axis, keepdims=True)
    spread_sq = jnp.mean(centred * centred, axis=axis, keepdims=True)
    return centred * lax.rsqrt(spread_sq + 1e-05)


def in_hbm(value):
    return pltpu.with_memory_space_constraint(value, pltpu.HBM)


def whole(shape):
    return pl.BlockSpec(shape, lambda *_: (0,) * len(shape))


def split(index, size):
    if size & (size - 1) == 0:
        return index >> (size.bit_length() - 1), index & (size - 1)
    return lax.div(index, size), lax.rem(index, size)


def pick(plan, want_far, half_ref, target_ref, listed, slots, counts):
    _, halves, nears, capacity = plan

    def none(tile, carry):
        counts[tile] = 0
        return carry

    def step(entry, count):
        target = target_ref[entry]
        rank = counts[target]
        counts[target] = rank + 1
        upper, near = split(target, nears)
        sec, half = split(upper, halves)
        listed[count] = entry
        slots[count] = (sec * nears + near) * capacity + rank
        far = (half != half_ref[0]).astype(jnp.int32)
        return count + (far if want_far else 1 - far)

    lax.fori_loop(0, counts.shape[0], none, 0)
    return lax.fori_loop(0, target_ref.shape[0], step, jnp.int32(0), unroll=4)


def multiply(plan, count, source_ref, block_ref, surface_ref, weights, listed, slots, made, labels, tile, out_ref, sems, tile_sem):
    capacity = plan[3]
    block = weights.shape[1]
    labels[...] = jnp.full_like(labels, -1)
    lane = lax.broadcasted_iota(jnp.int32, (1, labels.shape[1]), 1)

    def copy(at):
        peer, rank = split(slots[at], capacity)
        rows = pl.ds(pl.multiple_of(rank * block, block), block)
        return pltpu.make_async_copy(made.at[at], out_ref.at[peer, rows], sems.at[at])

    def group(size, first):
        for i in range(size):
            entry = listed[first + i]
            rows = pl.ds(pl.multiple_of(source_ref[entry] * block, block), block)
            made[first + i] = jnp.dot(
                weights[entry], surface_ref[rows, :], preferred_element_type=F32
            ).astype(BF16)
            peer, rank = split(slots[first + i], capacity)
            row = labels[pl.ds(peer, 1), :]
            labels[pl.ds(peer, 1), :] = jnp.where(lane == rank, block_ref[entry], row)
        for i in range(size):
            copy(first + i).start()

    def eight(i, carry):
        group(8, i * 8)
        return carry

    def one(i, carry):
        group(1, i)
        return carry

    def drain(i, carry):
        copy(i).wait()
        return carry

    full = count >> 3
    lax.fori_loop(0, full, eight, 0)
    lax.fori_loop(full * 8, count, one, 0)
    tile[...] = jnp.broadcast_to(labels[...].astype(F32)[:, None, :], tile.shape).astype(BF16)
    told = pltpu.make_async_copy(
        tile, out_ref.at[:, pl.ds(capacity * block, tile.shape[1])], tile_sem
    )
    told.start()
    lax.fori_loop(0, count, drain, 0)
    told.wait()


def remap_scratch(plan, entries, block, features):
    sections, halves, nears, _ = plan
    peers = sections * nears
    return [
        pltpu.SMEM((entries + 1,), jnp.int32),
        pltpu.SMEM((entries + 1,), jnp.int32),
        pltpu.SMEM((sections * halves * nears,), jnp.int32),
        pltpu.VMEM((entries, block, block), BF16),
        pltpu.VMEM((entries, block, features), BF16),
        pltpu.VMEM((peers, 128), jnp.int32),
        pltpu.VMEM((peers, 16, features), BF16),
        pltpu.SemaphoreType.DMA((entries,)),
        pltpu.SemaphoreType.DMA,
        pltpu.SemaphoreType.DMA,
    ]


def atm_kernel(
    plan,
    half_ref,
    target_ref,
    source_ref,
    block_ref,
    x_ref,
    gain_ref,
    up_ref,
    down_ref,
    flux_ref,
    weight_ref,
    next_ref,
    surface_ref,
    far_ref,
    normed,
    total,
    listed,
    slots,
    counts,
    weights,
    made,
    labels,
    tile,
    sems,
    tile_sem,
    weight_sem,
):
    step = pl.program_id(0)
    last = step == pl.num_programs(0) - 1
    parts = [slice(at, at + x_ref.shape[0] // 2) for at in (0, x_ref.shape[0] // 2)]
    fetch = pltpu.make_async_copy(weight_ref, weights, weight_sem)

    @pl.when(step == 0)
    def _():
        for rows in parts:
            values = x_ref[rows, :].astype(F32)
            normed[rows, :] = (normalised(values, -1) * gain_ref[...]).astype(BF16)
            total[rows, :] = values

    @pl.when(step == 1)
    def _():
        fetch.start()

    for rows in parts:
        raised = jnp.dot(normed[rows, :], up_ref[...], preferred_element_type=F32)
        hidden = gelu(raised.astype(BF16))
        total[rows, :] += jnp.dot(hidden, down_ref[...], preferred_element_type=F32)

    @pl.when(last)
    def _():
        for rows in parts:
            updated = total[rows, :].astype(BF16)
            next_ref[rows, :] = updated
            surface_ref[rows, :] = jnp.dot(
                updated, flux_ref[...], preferred_element_type=F32
            ).astype(BF16)
        count = pick(plan, True, half_ref, target_ref, listed, slots, counts)
        fetch.wait()
        multiply(plan, count, source_ref, block_ref, surface_ref, weights, listed, slots, made, labels, tile, far_ref, sems, tile_sem)


def atmosphere(plan, half, target, source, target_block, columns, gain, w_up, w_down, w_flux, weights):
    rows, width = columns.shape
    features = w_flux.shape[1]
    inner = w_up.shape[1]
    entries, block, _ = weights.shape
    part = inner // 4
    peers = plan[0] * plan[2]
    return pl.pallas_call(
        functools.partial(atm_kernel, plan),
        name="atmosphere",
        grid_spec=pltpu.PrefetchScalarGridSpec(
            num_scalar_prefetch=4,
            grid=(inner // part,),
            in_specs=[
                whole((rows, width)),
                whole((1, width)),
                pl.BlockSpec((width, part), lambda i, *_: (0, i)),
                pl.BlockSpec((part, width), lambda i, *_: (i, 0)),
                whole(w_flux.shape),
                pl.BlockSpec(memory_space=pltpu.HBM),
            ],
            out_specs=[
                whole((rows, width)),
                whole((rows, features)),
                pl.BlockSpec(memory_space=pltpu.HBM),
            ],
            scratch_shapes=[
                pltpu.VMEM((rows, width), BF16),
                pltpu.VMEM((rows, width), F32),
                *remap_scratch(plan, entries, block, features),
            ],
        ),
        out_shape=[
            pltpu.HBM((rows, width), BF16),
            pltpu.HBM((rows, features), BF16),
            pltpu.HBM((peers, plan[3] * block + 16, features), BF16),
        ],
        compiler_params=pltpu.CompilerParams(vmem_limit_bytes=56 << 20),
    )(
        half,
        target,
        source,
        target_block,
        in_hbm(columns),
        in_hbm(gain[None, :]),
        in_hbm(w_up),
        in_hbm(w_down),
        in_hbm(w_flux),
        in_hbm(weights),
    )


def near_kernel(
    plan,
    half_ref,
    target_ref,
    source_ref,
    block_ref,
    surface_ref,
    weight_ref,
    near_ref,
    listed,
    slots,
    counts,
    weights,
    made,
    labels,
    tile,
    sems,
    tile_sem,
    weight_sem,
):
    fetch = pltpu.make_async_copy(weight_ref, weights, weight_sem)
    fetch.start()
    count = pick(plan, False, half_ref, target_ref, listed, slots, counts)
    fetch.wait()
    multiply(plan, count, source_ref, block_ref, surface_ref, weights, listed, slots, made, labels, tile, near_ref, sems, tile_sem)


def near_remap(plan, half, target, source, target_block, surface, weights):
    entries, block, _ = weights.shape
    features = surface.shape[1]
    peers = plan[0] * plan[2]
    return pl.pallas_call(
        functools.partial(near_kernel, plan),
        name="near_remap",
        grid_spec=pltpu.PrefetchScalarGridSpec(
            num_scalar_prefetch=4,
            grid=(1,),
            in_specs=[whole(surface.shape), pl.BlockSpec(memory_space=pltpu.HBM)],
            out_specs=pl.BlockSpec(memory_space=pltpu.HBM),
            scratch_shapes=remap_scratch(plan, entries, block, features),
        ),
        out_shape=pltpu.HBM((peers, plan[3] * block + 16, features), BF16),
        compiler_params=pltpu.CompilerParams(vmem_limit_bytes=48 << 20),
    )(half, target, source, target_block, in_hbm(surface), in_hbm(weights))


def merge_kernel(capacity, arrived_ref, out_ref, arrived, tile, listed, labels, total, sems, tile_sem):
    peers = arrived.shape[0]
    block = out_ref.shape[1]

    def fetch(peer):
        return pltpu.make_async_copy(
            arrived_ref.at[peer, pl.ds(0, capacity * block)], arrived.at[peer], sems.at[peer]
        )

    told = pltpu.make_async_copy(
        arrived_ref.at[:, pl.ds(capacity * block, tile.shape[1])], tile, tile_sem
    )
    told.start()
    for peer in range(peers):
        fetch(peer).start()
    total[...] = jnp.zeros_like(total)
    told.wait()
    listed[...] = jnp.max(tile[...].astype(F32), axis=1).astype(jnp.int32)
    read = pltpu.make_async_copy(listed, labels, tile_sem)
    read.start()
    read.wait()

    def add(peer, carry):
        fetch(peer).wait()
        for rank in range(capacity):
            label = labels[peer, rank]

            @pl.when(label >= 0)
            def _():
                total[label] += arrived[peer, rank * block : (rank + 1) * block].astype(F32)

        return carry

    lax.fori_loop(0, peers, add, 0)
    out_ref[...] = total[...].astype(BF16)


def merged(capacity, arrived, blocks, block):
    peers, _, features = arrived.shape
    return pl.pallas_call(
        functools.partial(merge_kernel, capacity),
        name="merge",
        grid=(1,),
        in_specs=[pl.BlockSpec(memory_space=pltpu.HBM)],
        out_specs=whole((blocks, block, features)),
        scratch_shapes=[
            pltpu.VMEM((peers, capacity * block, features), BF16),
            pltpu.VMEM((peers, 16, features), BF16),
            pltpu.VMEM((peers, features), jnp.int32),
            pltpu.SMEM((peers, features), jnp.int32),
            pltpu.VMEM((blocks, block, features), F32),
            pltpu.SemaphoreType.DMA((peers,)),
            pltpu.SemaphoreType.DMA,
        ],
        out_shape=pltpu.HBM((blocks, block, features), BF16),
        compiler_params=pltpu.CompilerParams(vmem_limit_bytes=32 << 20),
    )(in_hbm(arrived))


def ocean_kernel(mix_ref, near_ref, far_ref, now_ref, sea_ref, force_ref, gain_ref, up_ref, down_ref, out_ref):
    forcing = (near_ref[...].astype(F32) + far_ref[...].astype(F32)).astype(BF16)
    driven = mix_ref[...] + lax.dot_general(
        force_ref[...], forcing, (((1,), (1,)), ((), ())), preferred_element_type=F32
    )
    normed = (normalised(driven, 0) * gain_ref[...]).astype(BF16)
    hidden = gelu(jnp.dot(up_ref[...], normed, preferred_element_type=F32).astype(BF16))
    change = jnp.dot(down_ref[...], hidden, preferred_element_type=F32)
    out_ref[...] = (
        now_ref[...].astype(F32) + sea_ref[...].astype(F32) * change
    ).astype(BF16)


def ocean(mixing, near, far, now, sea, w_force, gain, w_up, w_down):
    channels, cells = now.shape
    features = near.shape[1]
    part = cells // 5
    if part % 128:
        part = cells
    tall = pl.BlockSpec((channels, part), lambda i: (0, i))
    flat = pl.BlockSpec((part, features), lambda i: (i, 0))
    return pl.pallas_call(
        ocean_kernel,
        name="ocean",
        grid=(cells // part,),
        in_specs=[
            tall,
            flat,
            flat,
            tall,
            pl.BlockSpec((1, part), lambda i: (0, i)),
            whole(w_force.shape),
            whole((channels, 1)),
            whole(w_up.shape),
            whole(w_down.shape),
        ],
        out_specs=tall,
        out_shape=jax.ShapeDtypeStruct((channels, cells), BF16),
        compiler_params=pltpu.CompilerParams(vmem_limit_bytes=48 << 20),
    )(
        in_hbm(mixing),
        in_hbm(near),
        far,
        in_hbm(now),
        sea[None, :],
        w_force,
        gain[:, None],
        w_up,
        w_down,
    )


def edge_rows(block):
    count = math.prod(lax.axis_size(axis) for axis in ALL)
    forward = [(i, i + 1) for i in range(count - 1)]
    backward = [(target, source) for source, target in forward]
    low = lax.ppermute(block[:, -OX:], ALL, forward)
    high = lax.ppermute(block[:, :OX], ALL, backward)
    return low, high


def flat_mixing(padded_flat, kernel, row_len, cell_count):
    extended = jnp.pad(padded_flat.astype(F32), ((0, 0), (row_len, row_len)))
    column_at = (jnp.arange(cell_count, dtype=jnp.int32) % row_len)[None, :]
    first_col = column_at == 0
    last_col = column_at == row_len - 1

    def window(offset):
        return lax.slice_in_dim(extended, row_len + offset, row_len + offset + cell_count, axis=1)

    summed = jnp.zeros((padded_flat.shape[0], cell_count), F32)
    for row_step in range(3):
        base = row_step * row_len
        for col_step in range(3):
            if col_step == 0:
                shifted = jnp.where(first_col, window(base + row_len - 1), window(base - 1))
            elif col_step == 2:
                shifted = jnp.where(last_col, window(base - row_len + 1), window(base + 1))
            else:
                shifted = window(base)
            summed = summed + kernel[:, 3 * row_step + col_step][:, None] * shifted
    return summed


def local(
    atm_state,
    gain_atm,
    w_up_atm,
    w_down_atm,
    w_flux,
    ent_source,
    ent_target,
    ent_block,
    remap_weights,
    ocean_state,
    land_sea,
    conv_kernel,
    w_force,
    gain_ocn,
    w_up_ocn,
    w_down_ocn,
):
    sections, halves, nears = (lax.axis_size(axis) for axis in ALL)
    half = lax.axis_index("half")
    peers = sections * nears
    entries, block_rows, _ = remap_weights.shape
    capacity = max(2, 2 * entries // (peers * halves))
    cell_count = ocean_state.shape[1]
    ocean_blocks = cell_count // block_rows

    def exchange(values):
        return lax.all_to_all(values, PEERS, split_axis=0, concat_axis=0, tiled=True)

    plan = (sections, halves, nears, capacity)
    entry = (half[None], ent_target[:, 0], ent_source, ent_block)
    atm_next, surface, far_made = atmosphere(
        plan, *entry, atm_state, gain_atm, w_up_atm, w_down_atm, w_flux, remap_weights
    )
    low, high = edge_rows(ocean_state)
    far_made, low, high = lax.optimization_barrier((far_made, low, high))
    far_arrived = exchange(far_made)
    near_made = near_remap(plan, *entry, surface, remap_weights)
    padded = jnp.concatenate([low, ocean_state, high], axis=1)
    mixing = flat_mixing(padded, conv_kernel, OX, cell_count)
    far_arrived, near_made, mixing = lax.optimization_barrier((far_arrived, near_made, mixing))
    near_arrived = exchange(near_made)
    far_sum = merged(capacity, far_arrived, ocean_blocks, block_rows)
    far_sum = lax.ppermute(far_sum, "half", [(0, 1), (1, 0)])
    near_sum = merged(capacity, near_arrived, ocean_blocks, block_rows)
    features = far_sum.shape[2]
    ocean_next = ocean(
        mixing,
        near_sum.reshape(cell_count, features),
        far_sum.reshape(cell_count, features),
        ocean_state,
        land_sea,
        w_force.T,
        gain_ocn,
        w_up_ocn.T,
        w_down_ocn.T,
    )
    return (atm_next, ocean_next)


def solution(mesh):
    sections, tiles = mesh.shape["sec"], mesh.shape["tile"]
    fine = Mesh(mesh.devices.reshape(sections, 2, tiles // 2), ALL)
    placed = (
        P(ALL, None),
        P(),
        P(),
        P(),
        P(),
        P(ALL),
        P(ALL, None),
        P(ALL),
        P(ALL, None, None),
        P(None, ALL),
        P(ALL),
        P(),
        P(),
        P(),
        P(),
        P(),
    )
    return jax.shard_map(
        local,
        mesh=fine,
        in_specs=placed,
        out_specs=(P(ALL, None), P(None, ALL)),
        check_vma=False,
    )
```

```python
import functools
import math

import jax
import jax.numpy as jnp
from jax import lax
from jax.experimental import pallas as pl
from jax.experimental.pallas import tpu as pltpu
from jax.sharding import Mesh, PartitionSpec as P

OX = 1440
ALL = ("sec", "half", "near")
PEERS = ("sec", "near")
F32 = jnp.float32
BF16 = jnp.bfloat16


def gelu(x):
    half = 0.5 * x
    return half + half * jnp.tanh(x * (0.7978845608028654 + 0.035677408136300125 * (x * x)))


def normalised(values, axis):
    centred = values - jnp.mean(values, axis=axis, keepdims=True)
    spread_sq = jnp.mean(centred * centred, axis=axis, keepdims=True)
    return centred * lax.rsqrt(spread_sq + 1e-05)


def in_hbm(value):
    return pltpu.with_memory_space_constraint(value, pltpu.HBM)


def whole(shape):
    return pl.BlockSpec(shape, lambda *_: (0,) * len(shape))


def split(index, size):
    if size & (size - 1) == 0:
        return index >> (size.bit_length() - 1), index & (size - 1)
    return lax.div(index, size), lax.rem(index, size)


def pick(plan, want_far, half_ref, target_ref, listed, slots, counts):
    _, halves, nears, capacity = plan

    def none(tile, carry):
        counts[tile] = 0
        return carry

    def step(entry, count):
        target = target_ref[entry]
        rank = counts[target]
        counts[target] = rank + 1
        upper, near = split(target, nears)
        sec, half = split(upper, halves)
        listed[count] = entry
        slots[count] = (sec * nears + near) * capacity + rank
        far = (half != half_ref[0]).astype(jnp.int32)
        return count + (far if want_far else 1 - far)

    lax.fori_loop(0, counts.shape[0], none, 0)
    return lax.fori_loop(0, target_ref.shape[0], step, jnp.int32(0), unroll=4)


def multiply(plan, count, source_ref, block_ref, surface_ref, weights, listed, slots, made, labels, tile, out_ref, sems, tile_sem):
    capacity = plan[3]
    block = weights.shape[1]
    labels[...] = jnp.full_like(labels, -1)
    lane = lax.broadcasted_iota(jnp.int32, (1, labels.shape[1]), 1)

    def copy(at):
        peer, rank = split(slots[at], capacity)
        rows = pl.ds(pl.multiple_of(rank * block, block), block)
        return pltpu.make_async_copy(made.at[at], out_ref.at[peer, rows], sems.at[at])

    def group(size, first):
        for i in range(size):
            entry = listed[first + i]
            rows = pl.ds(pl.multiple_of(source_ref[entry] * block, block), block)
            made[first + i] = jnp.dot(
                weights[entry], surface_ref[rows, :], preferred_element_type=F32
            ).astype(BF16)
            peer, rank = split(slots[first + i], capacity)
            row = labels[pl.ds(peer, 1), :]
            labels[pl.ds(peer, 1), :] = jnp.where(lane == rank, block_ref[entry], row)
        for i in range(size):
            copy(first + i).start()

    def eight(i, carry):
        group(8, i * 8)
        return carry

    def one(i, carry):
        group(1, i)
        return carry

    def drain(i, carry):
        copy(i).wait()
        return carry

    full = count >> 3
    lax.fori_loop(0, full, eight, 0)
    lax.fori_loop(full * 8, count, one, 0)
    tile[...] = jnp.broadcast_to(labels[...].astype(F32)[:, None, :], tile.shape).astype(BF16)
    told = pltpu.make_async_copy(
        tile, out_ref.at[:, pl.ds(capacity * block, tile.shape[1])], tile_sem
    )
    told.start()
    lax.fori_loop(0, count, drain, 0)
    told.wait()


def remap_scratch(plan, entries, block, features):
    sections, halves, nears, _ = plan
    peers = sections * nears
    return [
        pltpu.SMEM((entries + 1,), jnp.int32),
        pltpu.SMEM((entries + 1,), jnp.int32),
        pltpu.SMEM((sections * halves * nears,), jnp.int32),
        pltpu.VMEM((entries, block, block), BF16),
        pltpu.VMEM((entries, block, features), BF16),
        pltpu.VMEM((peers, 128), jnp.int32),
        pltpu.VMEM((peers, 16, features), BF16),
        pltpu.SemaphoreType.DMA((entries,)),
        pltpu.SemaphoreType.DMA,
        pltpu.SemaphoreType.DMA,
    ]


def atm_kernel(
    plan,
    half_ref,
    target_ref,
    source_ref,
    block_ref,
    x_ref,
    gain_ref,
    up_ref,
    down_ref,
    flux_ref,
    weight_ref,
    next_ref,
    surface_ref,
    far_ref,
    normed,
    total,
    listed,
    slots,
    counts,
    weights,
    made,
    labels,
    tile,
    sems,
    tile_sem,
    weight_sem,
):
    step = pl.program_id(0)
    last = step == pl.num_programs(0) - 1
    parts = [slice(at, at + x_ref.shape[0] // 2) for at in (0, x_ref.shape[0] // 2)]
    fetch = pltpu.make_async_copy(weight_ref, weights, weight_sem)

    @pl.when(step == 0)
    def _():
        for rows in parts:
            values = x_ref[rows, :].astype(F32)
            normed[rows, :] = (normalised(values, -1) * gain_ref[...]).astype(BF16)
            total[rows, :] = values

    @pl.when(step == 1)
    def _():
        fetch.start()

    for rows in parts:
        raised = jnp.dot(normed[rows, :], up_ref[...], preferred_element_type=F32)
        hidden = gelu(raised.astype(BF16))
        total[rows, :] += jnp.dot(hidden, down_ref[...], preferred_element_type=F32)

    @pl.when(last)
    def _():
        for rows in parts:
            updated = total[rows, :].astype(BF16)
            next_ref[rows, :] = updated
            surface_ref[rows, :] = jnp.dot(
                updated, flux_ref[...], preferred_element_type=F32
            ).astype(BF16)
        count = pick(plan, True, half_ref, target_ref, listed, slots, counts)
        fetch.wait()
        multiply(plan, count, source_ref, block_ref, surface_ref, weights, listed, slots, made, labels, tile, far_ref, sems, tile_sem)


def atmosphere(plan, half, target, source, target_block, columns, gain, w_up, w_down, w_flux, weights):
    rows, width = columns.shape
    features = w_flux.shape[1]
    inner = w_up.shape[1]
    entries, block, _ = weights.shape
    part = inner // 4
    peers = plan[0] * plan[2]
    return pl.pallas_call(
        functools.partial(atm_kernel, plan),
        name="atmosphere",
        grid_spec=pltpu.PrefetchScalarGridSpec(
            num_scalar_prefetch=4,
            grid=(inner // part,),
            in_specs=[
                whole((rows, width)),
                whole((1, width)),
                pl.BlockSpec((width, part), lambda i, *_: (0, i)),
                pl.BlockSpec((part, width), lambda i, *_: (i, 0)),
                whole(w_flux.shape),
                pl.BlockSpec(memory_space=pltpu.HBM),
            ],
            out_specs=[
                whole((rows, width)),
                whole((rows, features)),
                pl.BlockSpec(memory_space=pltpu.HBM),
            ],
            scratch_shapes=[
                pltpu.VMEM((rows, width), BF16),
                pltpu.VMEM((rows, width), F32),
                *remap_scratch(plan, entries, block, features),
            ],
        ),
        out_shape=[
            pltpu.HBM((rows, width), BF16),
            pltpu.HBM((rows, features), BF16),
            pltpu.HBM((peers, plan[3] * block + 16, features), BF16),
        ],
        compiler_params=pltpu.CompilerParams(vmem_limit_bytes=56 << 20),
    )(
        half,
        target,
        source,
        target_block,
        in_hbm(columns),
        in_hbm(gain[None, :]),
        in_hbm(w_up),
        in_hbm(w_down),
        in_hbm(w_flux),
        in_hbm(weights),
    )


def near_kernel(
    plan,
    half_ref,
    target_ref,
    source_ref,
    block_ref,
    surface_ref,
    weight_ref,
    near_ref,
    listed,
    slots,
    counts,
    weights,
    made,
    labels,
    tile,
    sems,
    tile_sem,
    weight_sem,
):
    fetch = pltpu.make_async_copy(weight_ref, weights, weight_sem)
    fetch.start()
    count = pick(plan, False, half_ref, target_ref, listed, slots, counts)
    fetch.wait()
    multiply(plan, count, source_ref, block_ref, surface_ref, weights, listed, slots, made, labels, tile, near_ref, sems, tile_sem)


def near_remap(plan, half, target, source, target_block, surface, weights):
    entries, block, _ = weights.shape
    features = surface.shape[1]
    peers = plan[0] * plan[2]
    return pl.pallas_call(
        functools.partial(near_kernel, plan),
        name="near_remap",
        grid_spec=pltpu.PrefetchScalarGridSpec(
            num_scalar_prefetch=4,
            grid=(1,),
            in_specs=[whole(surface.shape), pl.BlockSpec(memory_space=pltpu.HBM)],
            out_specs=pl.BlockSpec(memory_space=pltpu.HBM),
            scratch_shapes=remap_scratch(plan, entries, block, features),
        ),
        out_shape=pltpu.HBM((peers, plan[3] * block + 16, features), BF16),
        compiler_params=pltpu.CompilerParams(vmem_limit_bytes=48 << 20),
    )(half, target, source, target_block, in_hbm(surface), in_hbm(weights))


def gather_slots(capacity, arrived_ref, arrived, tile, listed, labels, total, sems, tile_sem):
    peers = arrived.shape[0]
    block = total.shape[1]

    def fetch(peer):
        return pltpu.make_async_copy(
            arrived_ref.at[peer, pl.ds(0, capacity * block)], arrived.at[peer], sems.at[peer]
        )

    told = pltpu.make_async_copy(
        arrived_ref.at[:, pl.ds(capacity * block, tile.shape[1])], tile, tile_sem
    )
    told.start()
    for peer in range(peers):
        fetch(peer).start()
    total[...] = jnp.zeros_like(total)
    told.wait()
    listed[...] = jnp.max(tile[...].astype(F32), axis=1).astype(jnp.int32)
    read = pltpu.make_async_copy(listed, labels, tile_sem)
    read.start()
    read.wait()

    def add(peer, carry):
        fetch(peer).wait()
        for rank in range(capacity):
            label = labels[peer, rank]

            @pl.when(label >= 0)
            def _():
                total[label] += arrived[peer, rank * block : (rank + 1) * block].astype(F32)

        return carry

    lax.fori_loop(0, peers, add, 0)


def gather_scratch(peers, capacity, blocks, block, features):
    return [
        pltpu.VMEM((peers, capacity * block, features), BF16),
        pltpu.VMEM((peers, 16, features), BF16),
        pltpu.VMEM((peers, features), jnp.int32),
        pltpu.SMEM((peers, features), jnp.int32),
        pltpu.VMEM((blocks, block, features), F32),
        pltpu.SemaphoreType.DMA((peers,)),
        pltpu.SemaphoreType.DMA,
    ]


def merge_kernel(capacity, arrived_ref, out_ref, arrived, tile, listed, labels, total, sems, tile_sem):
    gather_slots(capacity, arrived_ref, arrived, tile, listed, labels, total, sems, tile_sem)
    out_ref[...] = total[...].astype(BF16)


def merged(capacity, arrived, blocks, block):
    peers, _, features = arrived.shape
    return pl.pallas_call(
        functools.partial(merge_kernel, capacity),
        name="merge",
        grid=(1,),
        in_specs=[pl.BlockSpec(memory_space=pltpu.HBM)],
        out_specs=whole((blocks, block, features)),
        scratch_shapes=gather_scratch(peers, capacity, blocks, block, features),
        out_shape=pltpu.HBM((blocks, block, features), BF16),
        compiler_params=pltpu.CompilerParams(vmem_limit_bytes=32 << 20),
    )(in_hbm(arrived))


def ocean_kernel(
    capacity,
    mix_ref,
    near_ref,
    far_ref,
    now_ref,
    sea_ref,
    force_ref,
    gain_ref,
    up_ref,
    down_ref,
    out_ref,
    arrived,
    tile,
    listed,
    labels,
    total,
    sems,
    tile_sem,
):
    step = pl.program_id(0)

    @pl.when(step == 0)
    def _():
        gather_slots(capacity, near_ref, arrived, tile, listed, labels, total, sems, tile_sem)

    blocks = far_ref.shape[0]
    forcing = (total[pl.ds(step * blocks, blocks)] + far_ref[...].astype(F32)).astype(BF16)
    forcing = forcing.reshape(blocks * forcing.shape[1], forcing.shape[2])
    driven = mix_ref[...].astype(F32) + lax.dot_general(
        force_ref[...], forcing, (((1,), (1,)), ((), ())), preferred_element_type=F32
    )
    normed = (normalised(driven, 0) * gain_ref[...]).astype(BF16)
    hidden = gelu(jnp.dot(up_ref[...], normed, preferred_element_type=F32).astype(BF16))
    change = jnp.dot(down_ref[...], hidden, preferred_element_type=F32)
    out_ref[...] = (now_ref[...].astype(F32) + sea_ref[...].astype(F32) * change).astype(BF16)


def ocean(capacity, mixing, near, far, now, sea, w_force, gain, w_up, w_down):
    channels, cells = now.shape
    blocks, block, features = far.shape
    peers = near.shape[0]
    steps = 5 if blocks % 5 == 0 else 1
    part = cells // steps
    tall = pl.BlockSpec((channels, part), lambda i: (0, i))
    return pl.pallas_call(
        functools.partial(ocean_kernel, capacity),
        name="ocean",
        grid=(steps,),
        in_specs=[
            tall,
            pl.BlockSpec(memory_space=pltpu.HBM),
            pl.BlockSpec((blocks // steps, block, features), lambda i: (i, 0, 0)),
            tall,
            pl.BlockSpec((1, part), lambda i: (0, i)),
            whole(w_force.shape),
            whole((channels, 1)),
            whole(w_up.shape),
            whole(w_down.shape),
        ],
        out_specs=tall,
        out_shape=jax.ShapeDtypeStruct((channels, cells), BF16),
        scratch_shapes=gather_scratch(peers, capacity, blocks, block, features),
        compiler_params=pltpu.CompilerParams(vmem_limit_bytes=48 << 20),
    )(
        in_hbm(mixing),
        in_hbm(near),
        far,
        in_hbm(now),
        sea[None, :],
        w_force,
        gain[:, None],
        w_up,
        w_down,
    )


def edge_rows(block):
    count = math.prod(lax.axis_size(axis) for axis in ALL)
    forward = [(i, i + 1) for i in range(count - 1)]
    backward = [(target, source) for source, target in forward]
    low = lax.ppermute(block[:, -OX:], ALL, forward)
    high = lax.ppermute(block[:, :OX], ALL, backward)
    return low, high


def flat_mixing(padded_flat, kernel, row_len, cell_count):
    extended = jnp.pad(padded_flat.astype(F32), ((0, 0), (row_len, row_len)))
    column_at = (jnp.arange(cell_count, dtype=jnp.int32) % row_len)[None, :]
    first_col = column_at == 0
    last_col = column_at == row_len - 1

    def window(offset):
        return lax.slice_in_dim(extended, row_len + offset, row_len + offset + cell_count, axis=1)

    summed = jnp.zeros((padded_flat.shape[0], cell_count), F32)
    for row_step in range(3):
        base = row_step * row_len
        for col_step in range(3):
            if col_step == 0:
                shifted = jnp.where(first_col, window(base + row_len - 1), window(base - 1))
            elif col_step == 2:
                shifted = jnp.where(last_col, window(base - row_len + 1), window(base + 1))
            else:
                shifted = window(base)
            summed = summed + kernel[:, 3 * row_step + col_step][:, None] * shifted
    return summed


def local(
    atm_state,
    gain_atm,
    w_up_atm,
    w_down_atm,
    w_flux,
    ent_source,
    ent_target,
    ent_block,
    remap_weights,
    ocean_state,
    land_sea,
    conv_kernel,
    w_force,
    gain_ocn,
    w_up_ocn,
    w_down_ocn,
):
    sections, halves, nears = (lax.axis_size(axis) for axis in ALL)
    half = lax.axis_index("half")
    peers = sections * nears
    entries, block_rows, _ = remap_weights.shape
    capacity = max(2, 2 * entries // (peers * halves))
    cell_count = ocean_state.shape[1]
    ocean_blocks = cell_count // block_rows

    def exchange(values):
        return lax.all_to_all(values, PEERS, split_axis=0, concat_axis=0, tiled=True)

    plan = (sections, halves, nears, capacity)
    entry = (half[None], ent_target[:, 0], ent_source, ent_block)
    atm_next, surface, far_made = atmosphere(
        plan, *entry, atm_state, gain_atm, w_up_atm, w_down_atm, w_flux, remap_weights
    )
    low, high = edge_rows(ocean_state)
    far_made, low, high = lax.optimization_barrier((far_made, low, high))
    far_arrived = exchange(far_made)
    near_made = near_remap(plan, *entry, surface, remap_weights)
    padded = jnp.concatenate([low, ocean_state, high], axis=1)
    mixing = flat_mixing(padded, conv_kernel, OX, cell_count).astype(BF16)
    far_arrived, near_made, mixing = lax.optimization_barrier((far_arrived, near_made, mixing))
    near_arrived = exchange(near_made)
    far_sum = merged(capacity, far_arrived, ocean_blocks, block_rows)
    far_sum = lax.ppermute(far_sum, "half", [(0, 1), (1, 0)])
    ocean_next = ocean(
        capacity,
        mixing,
        near_arrived,
        far_sum,
        ocean_state,
        land_sea,
        w_force.T,
        gain_ocn,
        w_up_ocn.T,
        w_down_ocn.T,
    )
    return (atm_next, ocean_next)


def solution(mesh):
    sections, tiles = mesh.shape["sec"], mesh.shape["tile"]
    fine = Mesh(mesh.devices.reshape(sections, 2, tiles // 2), ALL)
    placed = (
        P(ALL, None),
        P(),
        P(),
        P(),
        P(),
        P(ALL),
        P(ALL, None),
        P(ALL),
        P(ALL, None, None),
        P(None, ALL),
        P(ALL),
        P(),
        P(),
        P(),
        P(),
        P(),
    )
    return jax.shard_map(
        local,
        mesh=fine,
        in_specs=placed,
        out_specs=(P(ALL, None), P(None, ALL)),
        check_vma=False,
    )
```

```python
import functools
import math

import jax
import jax.numpy as jnp
from jax import lax
from jax.experimental import pallas as pl
from jax.experimental.pallas import tpu as pltpu
from jax.sharding import Mesh, PartitionSpec as P

OX = 1440
ALL = ("sec", "half", "near")
PEERS = ("sec", "near")
F32 = jnp.float32
BF16 = jnp.bfloat16


def gelu(x):
    half = 0.5 * x
    return half + half * jnp.tanh(x * (0.7978845608028654 + 0.035677408136300125 * (x * x)))


def normalised(values, axis):
    centred = values - jnp.mean(values, axis=axis, keepdims=True)
    spread_sq = jnp.mean(centred * centred, axis=axis, keepdims=True)
    return centred * lax.rsqrt(spread_sq + 1e-05)


def in_hbm(value):
    return pltpu.with_memory_space_constraint(value, pltpu.HBM)


def in_vmem(value):
    return pltpu.with_memory_space_constraint(value, pltpu.VMEM)


def whole(shape):
    return pl.BlockSpec(shape, lambda *_: (0,) * len(shape))


def split(index, size):
    if size & (size - 1) == 0:
        return index >> (size.bit_length() - 1), index & (size - 1)
    return lax.div(index, size), lax.rem(index, size)


def pick(plan, want_far, half_ref, target_ref, listed, slots, counts):
    _, halves, nears, capacity = plan

    def none(tile, carry):
        counts[tile] = 0
        return carry

    def step(entry, count):
        target = target_ref[entry]
        rank = counts[target]
        counts[target] = rank + 1
        upper, near = split(target, nears)
        sec, half = split(upper, halves)
        listed[count] = entry
        slots[count] = (sec * nears + near) * capacity + rank
        far = (half != half_ref[0]).astype(jnp.int32)
        return count + (far if want_far else 1 - far)

    lax.fori_loop(0, counts.shape[0], none, 0)
    return lax.fori_loop(0, target_ref.shape[0], step, jnp.int32(0), unroll=4)


def multiply(plan, count, source_ref, block_ref, surface_ref, weights, listed, slots, made, labels, tile, out_ref, sems, tile_sem):
    capacity = plan[3]
    block = weights.shape[1]
    labels[...] = jnp.full_like(labels, -1)
    lane = lax.broadcasted_iota(jnp.int32, (1, labels.shape[1]), 1)

    def copy(at):
        peer, rank = split(slots[at], capacity)
        rows = pl.ds(pl.multiple_of(rank * block, block), block)
        return pltpu.make_async_copy(made.at[at], out_ref.at[peer, rows], sems.at[at])

    def group(size, first):
        for i in range(size):
            entry = listed[first + i]
            rows = pl.ds(pl.multiple_of(source_ref[entry] * block, block), block)
            made[first + i] = jnp.dot(
                weights[entry], surface_ref[rows, :], preferred_element_type=F32
            ).astype(BF16)
            peer, rank = split(slots[first + i], capacity)
            row = labels[pl.ds(peer, 1), :]
            labels[pl.ds(peer, 1), :] = jnp.where(lane == rank, block_ref[entry], row)
        for i in range(size):
            copy(first + i).start()

    def eight(i, carry):
        group(8, i * 8)
        return carry

    def one(i, carry):
        group(1, i)
        return carry

    def drain(i, carry):
        copy(i).wait()
        return carry

    full = count >> 3
    lax.fori_loop(0, full, eight, 0)
    lax.fori_loop(full * 8, count, one, 0)
    tile[...] = jnp.broadcast_to(labels[...].astype(F32)[:, None, :], tile.shape).astype(BF16)
    told = pltpu.make_async_copy(
        tile, out_ref.at[:, pl.ds(capacity * block, tile.shape[1])], tile_sem
    )
    told.start()
    lax.fori_loop(0, count, drain, 0)
    told.wait()


def remap_scratch(plan, entries, block, features):
    sections, halves, nears, _ = plan
    peers = sections * nears
    return [
        pltpu.SMEM((entries + 1,), jnp.int32),
        pltpu.SMEM((entries + 1,), jnp.int32),
        pltpu.SMEM((sections * halves * nears,), jnp.int32),
        pltpu.VMEM((entries, block, block), BF16),
        pltpu.VMEM((entries, block, features), BF16),
        pltpu.VMEM((peers, 128), jnp.int32),
        pltpu.VMEM((peers, 16, features), BF16),
        pltpu.SemaphoreType.DMA((entries,)),
        pltpu.SemaphoreType.DMA,
        pltpu.SemaphoreType.DMA,
    ]


def atm_kernel(
    plan,
    half_ref,
    target_ref,
    source_ref,
    block_ref,
    x_ref,
    gain_ref,
    up_ref,
    down_ref,
    flux_ref,
    weight_ref,
    next_ref,
    surface_ref,
    far_ref,
    normed,
    total,
    listed,
    slots,
    counts,
    weights,
    made,
    labels,
    tile,
    sems,
    tile_sem,
    weight_sem,
):
    step = pl.program_id(0)
    last = step == pl.num_programs(0) - 1
    parts = [slice(at, at + x_ref.shape[0] // 2) for at in (0, x_ref.shape[0] // 2)]
    fetch = pltpu.make_async_copy(weight_ref, weights, weight_sem)

    @pl.when(step == 0)
    def _():
        for rows in parts:
            values = x_ref[rows, :].astype(F32)
            normed[rows, :] = (normalised(values, -1) * gain_ref[...]).astype(BF16)
            total[rows, :] = values

    @pl.when(step == 1)
    def _():
        fetch.start()

    for rows in parts:
        raised = jnp.dot(normed[rows, :], up_ref[...], preferred_element_type=F32)
        hidden = gelu(raised.astype(BF16))
        total[rows, :] += jnp.dot(hidden, down_ref[...], preferred_element_type=F32)

    @pl.when(last)
    def _():
        for rows in parts:
            updated = total[rows, :].astype(BF16)
            next_ref[rows, :] = updated
            surface_ref[rows, :] = jnp.dot(
                updated, flux_ref[...], preferred_element_type=F32
            ).astype(BF16)
        count = pick(plan, True, half_ref, target_ref, listed, slots, counts)
        fetch.wait()
        multiply(plan, count, source_ref, block_ref, surface_ref, weights, listed, slots, made, labels, tile, far_ref, sems, tile_sem)


def atmosphere(plan, half, target, source, target_block, columns, gain, w_up, w_down, w_flux, weights):
    rows, width = columns.shape
    features = w_flux.shape[1]
    inner = w_up.shape[1]
    entries, block, _ = weights.shape
    part = inner // 4
    peers = plan[0] * plan[2]
    return pl.pallas_call(
        functools.partial(atm_kernel, plan),
        name="atmosphere",
        grid_spec=pltpu.PrefetchScalarGridSpec(
            num_scalar_prefetch=4,
            grid=(inner // part,),
            in_specs=[
                whole((rows, width)),
                whole((1, width)),
                pl.BlockSpec((width, part), lambda i, *_: (0, i)),
                pl.BlockSpec((part, width), lambda i, *_: (i, 0)),
                whole(w_flux.shape),
                pl.BlockSpec(memory_space=pltpu.HBM),
            ],
            out_specs=[
                whole((rows, width)),
                whole((rows, features)),
                pl.BlockSpec(memory_space=pltpu.HBM),
            ],
            scratch_shapes=[
                pltpu.VMEM((rows, width), BF16),
                pltpu.VMEM((rows, width), F32),
                *remap_scratch(plan, entries, block, features),
            ],
        ),
        out_shape=[
            pltpu.HBM((rows, width), BF16),
            pltpu.HBM((rows, features), BF16),
            pltpu.HBM((peers, plan[3] * block + 16, features), BF16),
        ],
        compiler_params=pltpu.CompilerParams(vmem_limit_bytes=56 << 20),
    )(
        half,
        target,
        source,
        target_block,
        in_hbm(columns),
        in_hbm(gain[None, :]),
        in_hbm(w_up),
        in_hbm(w_down),
        in_hbm(w_flux),
        in_hbm(weights),
    )


def near_kernel(
    plan,
    half_ref,
    target_ref,
    source_ref,
    block_ref,
    surface_ref,
    weight_ref,
    near_ref,
    listed,
    slots,
    counts,
    weights,
    made,
    labels,
    tile,
    sems,
    tile_sem,
    weight_sem,
):
    fetch = pltpu.make_async_copy(weight_ref, weights, weight_sem)
    fetch.start()
    count = pick(plan, False, half_ref, target_ref, listed, slots, counts)
    fetch.wait()
    multiply(plan, count, source_ref, block_ref, surface_ref, weights, listed, slots, made, labels, tile, near_ref, sems, tile_sem)


def near_remap(plan, half, target, source, target_block, surface, weights):
    entries, block, _ = weights.shape
    features = surface.shape[1]
    peers = plan[0] * plan[2]
    return pl.pallas_call(
        functools.partial(near_kernel, plan),
        name="near_remap",
        grid_spec=pltpu.PrefetchScalarGridSpec(
            num_scalar_prefetch=4,
            grid=(1,),
            in_specs=[whole(surface.shape), pl.BlockSpec(memory_space=pltpu.HBM)],
            out_specs=pl.BlockSpec(memory_space=pltpu.HBM),
            scratch_shapes=remap_scratch(plan, entries, block, features),
        ),
        out_shape=pltpu.HBM((peers, plan[3] * block + 16, features), BF16),
        compiler_params=pltpu.CompilerParams(vmem_limit_bytes=48 << 20),
    )(half, target, source, target_block, in_hbm(surface), in_hbm(weights))


def merge_kernel(capacity, arrived_ref, out_ref, arrived, tile, listed, labels, total, sems, tile_sem):
    peers = arrived.shape[0]
    block = out_ref.shape[1]

    def fetch(peer):
        return pltpu.make_async_copy(
            arrived_ref.at[peer, pl.ds(0, capacity * block)], arrived.at[peer], sems.at[peer]
        )

    told = pltpu.make_async_copy(
        arrived_ref.at[:, pl.ds(capacity * block, tile.shape[1])], tile, tile_sem
    )
    told.start()
    for peer in range(peers):
        fetch(peer).start()
    total[...] = jnp.zeros_like(total)
    told.wait()
    listed[...] = jnp.max(tile[...].astype(F32), axis=1).astype(jnp.int32)
    read = pltpu.make_async_copy(listed, labels, tile_sem)
    read.start()
    read.wait()

    def add(peer, carry):
        fetch(peer).wait()
        for rank in range(capacity):
            label = labels[peer, rank]

            @pl.when(label >= 0)
            def _():
                total[label] += arrived[peer, rank * block : (rank + 1) * block].astype(F32)

        return carry

    lax.fori_loop(0, peers, add, 0)
    out_ref[...] = total[...].astype(BF16)


def merged(capacity, arrived, blocks, block):
    peers, _, features = arrived.shape
    return pl.pallas_call(
        functools.partial(merge_kernel, capacity),
        name="merge",
        grid=(1,),
        in_specs=[pl.BlockSpec(memory_space=pltpu.HBM)],
        out_specs=whole((blocks, block, features)),
        scratch_shapes=[
            pltpu.VMEM((peers, capacity * block, features), BF16),
            pltpu.VMEM((peers, 16, features), BF16),
            pltpu.VMEM((peers, features), jnp.int32),
            pltpu.SMEM((peers, features), jnp.int32),
            pltpu.VMEM((blocks, block, features), F32),
            pltpu.SemaphoreType.DMA((peers,)),
            pltpu.SemaphoreType.DMA,
        ],
        out_shape=jax.ShapeDtypeStruct((blocks, block, features), BF16),
        compiler_params=pltpu.CompilerParams(vmem_limit_bytes=32 << 20),
    )(in_hbm(arrived))


def ocean_kernel(mix_ref, near_ref, far_ref, now_ref, sea_ref, force_ref, gain_ref, up_ref, down_ref, out_ref):
    forcing = (near_ref[...].astype(F32) + far_ref[...].astype(F32)).astype(BF16)
    driven = mix_ref[...].astype(F32) + lax.dot_general(
        force_ref[...], forcing, (((1,), (1,)), ((), ())), preferred_element_type=F32
    )
    normed = (normalised(driven, 0) * gain_ref[...]).astype(BF16)
    hidden = gelu(jnp.dot(up_ref[...], normed, preferred_element_type=F32).astype(BF16))
    change = jnp.dot(down_ref[...], hidden, preferred_element_type=F32)
    out_ref[...] = (
        now_ref[...].astype(F32) + sea_ref[...].astype(F32) * change
    ).astype(BF16)


def ocean(mixing, near, far, now, sea, w_force, gain, w_up, w_down):
    channels, cells = now.shape
    features = near.shape[1]
    part = cells // 3
    if part % 128:
        part = cells
    tall = pl.BlockSpec((channels, part), lambda i: (0, i))
    flat = pl.BlockSpec((part, features), lambda i: (i, 0))
    return pl.pallas_call(
        ocean_kernel,
        name="ocean",
        grid=(cells // part,),
        in_specs=[
            tall,
            flat,
            flat,
            tall,
            pl.BlockSpec((1, part), lambda i: (0, i)),
            whole(w_force.shape),
            whole((channels, 1)),
            whole(w_up.shape),
            whole(w_down.shape),
        ],
        out_specs=tall,
        out_shape=jax.ShapeDtypeStruct((channels, cells), BF16),
        compiler_params=pltpu.CompilerParams(vmem_limit_bytes=32 << 20),
    )(
        in_vmem(mixing),
        in_vmem(near),
        in_vmem(far),
        in_vmem(now),
        in_vmem(sea[None, :]),
        in_vmem(w_force),
        in_vmem(gain[:, None]),
        in_vmem(w_up),
        in_vmem(w_down),
    )


def edge_rows(block):
    count = math.prod(lax.axis_size(axis) for axis in ALL)
    forward = [(i, i + 1) for i in range(count - 1)]
    backward = [(target, source) for source, target in forward]
    low = lax.ppermute(block[:, -OX:], ALL, forward)
    high = lax.ppermute(block[:, :OX], ALL, backward)
    return low, high


def flat_mixing(padded_flat, kernel, row_len, cell_count):
    extended = jnp.pad(padded_flat.astype(F32), ((0, 0), (row_len, row_len)))
    column_at = (jnp.arange(cell_count, dtype=jnp.int32) % row_len)[None, :]
    first_col = column_at == 0
    last_col = column_at == row_len - 1

    def window(offset):
        return lax.slice_in_dim(extended, row_len + offset, row_len + offset + cell_count, axis=1)

    summed = jnp.zeros((padded_flat.shape[0], cell_count), F32)
    for row_step in range(3):
        base = row_step * row_len
        for col_step in range(3):
            if col_step == 0:
                shifted = jnp.where(first_col, window(base + row_len - 1), window(base - 1))
            elif col_step == 2:
                shifted = jnp.where(last_col, window(base - row_len + 1), window(base + 1))
            else:
                shifted = window(base)
            summed = summed + kernel[:, 3 * row_step + col_step][:, None] * shifted
    return summed


def local(
    atm_state,
    gain_atm,
    w_up_atm,
    w_down_atm,
    w_flux,
    ent_source,
    ent_target,
    ent_block,
    remap_weights,
    ocean_state,
    land_sea,
    conv_kernel,
    w_force,
    gain_ocn,
    w_up_ocn,
    w_down_ocn,
):
    sections, halves, nears = (lax.axis_size(axis) for axis in ALL)
    half = lax.axis_index("half")
    peers = sections * nears
    entries, block_rows, _ = remap_weights.shape
    capacity = max(2, 2 * entries // (peers * halves))
    cell_count = ocean_state.shape[1]
    ocean_blocks = cell_count // block_rows

    def exchange(values):
        return lax.all_to_all(values, PEERS, split_axis=0, concat_axis=0, tiled=True)

    plan = (sections, halves, nears, capacity)
    entry = (half[None], ent_target[:, 0], ent_source, ent_block)
    atm_next, surface, far_made = atmosphere(
        plan, *entry, atm_state, gain_atm, w_up_atm, w_down_atm, w_flux, remap_weights
    )
    low, high = edge_rows(ocean_state)
    far_made, low, high = lax.optimization_barrier((far_made, low, high))
    far_arrived = exchange(far_made)
    near_made = near_remap(plan, *entry, surface, remap_weights)
    padded = jnp.concatenate([low, ocean_state, high], axis=1)
    mixing = flat_mixing(padded, conv_kernel, OX, cell_count).astype(BF16)
    far_arrived, near_made, mixing = lax.optimization_barrier((far_arrived, near_made, mixing))
    near_arrived = exchange(near_made)
    far_sum = merged(capacity, far_arrived, ocean_blocks, block_rows)
    far_sum = lax.ppermute(far_sum, "half", [(0, 1), (1, 0)])
    near_sum = merged(capacity, near_arrived, ocean_blocks, block_rows)
    features = far_sum.shape[2]
    ocean_next = ocean(
        mixing,
        near_sum.reshape(cell_count, features),
        far_sum.reshape(cell_count, features),
        ocean_state,
        land_sea,
        w_force.T,
        gain_ocn,
        w_up_ocn.T,
        w_down_ocn.T,
    )
    return (atm_next, ocean_next)


def solution(mesh):
    sections, tiles = mesh.shape["sec"], mesh.shape["tile"]
    fine = Mesh(mesh.devices.reshape(sections, 2, tiles // 2), ALL)
    placed = (
        P(ALL, None),
        P(),
        P(),
        P(),
        P(),
        P(ALL),
        P(ALL, None),
        P(ALL),
        P(ALL, None, None),
        P(None, ALL),
        P(ALL),
        P(),
        P(),
        P(),
        P(),
        P(),
    )
    return jax.shard_map(
        local,
        mesh=fine,
        in_specs=placed,
        out_specs=(P(ALL, None), P(None, ALL)),
        check_vma=False,
    )
```

```python
import functools
import math

import jax
import jax.numpy as jnp
from jax import lax
from jax.experimental import pallas as pl
from jax.experimental.pallas import tpu as pltpu
from jax.sharding import Mesh, PartitionSpec as P

OX = 1440
ALL = ("sec", "half", "near")
PEERS = ("sec", "near")
F32 = jnp.float32
BF16 = jnp.bfloat16


def gelu(x):
    half = 0.5 * x
    return half + half * jnp.tanh(x * (0.7978845608028654 + 0.035677408136300125 * (x * x)))


def normalised(values, axis):
    centred = values - jnp.mean(values, axis=axis, keepdims=True)
    spread_sq = jnp.mean(centred * centred, axis=axis, keepdims=True)
    return centred * lax.rsqrt(spread_sq + 1e-05)


def in_hbm(value):
    return pltpu.with_memory_space_constraint(value, pltpu.HBM)


def in_vmem(value):
    return pltpu.with_memory_space_constraint(value, pltpu.VMEM)


def whole(shape):
    return pl.BlockSpec(shape, lambda *_: (0,) * len(shape))


def split(index, size):
    if size & (size - 1) == 0:
        return index >> (size.bit_length() - 1), index & (size - 1)
    return lax.div(index, size), lax.rem(index, size)


def pick(plan, want_far, half_ref, target_ref, listed, slots, counts):
    _, halves, nears, capacity = plan

    def none(tile, carry):
        counts[tile] = 0
        return carry

    def step(entry, count):
        target = target_ref[entry]
        rank = counts[target]
        counts[target] = rank + 1
        upper, near = split(target, nears)
        sec, half = split(upper, halves)
        listed[count] = entry
        slots[count] = (sec * nears + near) * capacity + rank
        far = (half != half_ref[0]).astype(jnp.int32)
        return count + (far if want_far else 1 - far)

    lax.fori_loop(0, counts.shape[0], none, 0)
    return lax.fori_loop(0, target_ref.shape[0], step, jnp.int32(0), unroll=4)


def multiply(plan, count, source_ref, block_ref, surface_ref, weights, listed, slots, made, labels, tile, out_ref, sems, tile_sem):
    capacity = plan[3]
    block = weights.shape[1]
    labels[...] = jnp.full_like(labels, -1)
    lane = lax.broadcasted_iota(jnp.int32, (1, labels.shape[1]), 1)

    def copy(at):
        peer, rank = split(slots[at], capacity)
        rows = pl.ds(pl.multiple_of(rank * block, block), block)
        return pltpu.make_async_copy(made.at[at], out_ref.at[peer, rows], sems.at[at])

    def group(size, first):
        for i in range(size):
            entry = listed[first + i]
            rows = pl.ds(pl.multiple_of(source_ref[entry] * block, block), block)
            made[first + i] = jnp.dot(
                weights[entry], surface_ref[rows, :], preferred_element_type=F32
            ).astype(BF16)
            peer, rank = split(slots[first + i], capacity)
            row = labels[pl.ds(peer, 1), :]
            labels[pl.ds(peer, 1), :] = jnp.where(lane == rank, block_ref[entry], row)
        for i in range(size):
            copy(first + i).start()

    def eight(i, carry):
        group(8, i * 8)
        return carry

    def one(i, carry):
        group(1, i)
        return carry

    def drain(i, carry):
        copy(i).wait()
        return carry

    full = count >> 3
    lax.fori_loop(0, full, eight, 0)
    lax.fori_loop(full * 8, count, one, 0)
    tile[...] = jnp.broadcast_to(labels[...].astype(F32)[:, None, :], tile.shape).astype(BF16)
    told = pltpu.make_async_copy(
        tile, out_ref.at[:, pl.ds(capacity * block, tile.shape[1])], tile_sem
    )
    told.start()
    lax.fori_loop(0, count, drain, 0)
    told.wait()


def remap_scratch(plan, entries, block, features):
    sections, halves, nears, _ = plan
    peers = sections * nears
    return [
        pltpu.SMEM((entries + 1,), jnp.int32),
        pltpu.SMEM((entries + 1,), jnp.int32),
        pltpu.SMEM((sections * halves * nears,), jnp.int32),
        pltpu.VMEM((entries, block, block), BF16),
        pltpu.VMEM((entries, block, features), BF16),
        pltpu.VMEM((peers, 128), jnp.int32),
        pltpu.VMEM((peers, 16, features), BF16),
        pltpu.SemaphoreType.DMA((entries,)),
        pltpu.SemaphoreType.DMA,
        pltpu.SemaphoreType.DMA,
    ]


def atm_kernel(
    plan,
    half_ref,
    target_ref,
    source_ref,
    block_ref,
    x_ref,
    gain_ref,
    up_ref,
    down_ref,
    flux_ref,
    weight_ref,
    next_ref,
    surface_ref,
    far_ref,
    normed,
    total,
    listed,
    slots,
    counts,
    weights,
    made,
    labels,
    tile,
    sems,
    tile_sem,
    weight_sem,
):
    step = pl.program_id(0)
    last = step == pl.num_programs(0) - 1
    parts = [slice(at, at + x_ref.shape[0] // 2) for at in (0, x_ref.shape[0] // 2)]
    fetch = pltpu.make_async_copy(weight_ref, weights, weight_sem)

    @pl.when(step == 0)
    def _():
        for rows in parts:
            values = x_ref[rows, :].astype(F32)
            normed[rows, :] = (normalised(values, -1) * gain_ref[...]).astype(BF16)
            total[rows, :] = values

    @pl.when(step == 1)
    def _():
        fetch.start()

    for rows in parts:
        raised = jnp.dot(normed[rows, :], up_ref[...], preferred_element_type=F32)
        hidden = gelu(raised.astype(BF16))
        total[rows, :] += jnp.dot(hidden, down_ref[...], preferred_element_type=F32)

    @pl.when(last)
    def _():
        for rows in parts:
            updated = total[rows, :].astype(BF16)
            next_ref[rows, :] = updated
            surface_ref[rows, :] = jnp.dot(
                updated, flux_ref[...], preferred_element_type=F32
            ).astype(BF16)
        count = pick(plan, True, half_ref, target_ref, listed, slots, counts)
        fetch.wait()
        multiply(plan, count, source_ref, block_ref, surface_ref, weights, listed, slots, made, labels, tile, far_ref, sems, tile_sem)


def atmosphere(plan, half, target, source, target_block, columns, gain, w_up, w_down, w_flux, weights):
    rows, width = columns.shape
    features = w_flux.shape[1]
    inner = w_up.shape[1]
    entries, block, _ = weights.shape
    part = inner // 4
    peers = plan[0] * plan[2]
    return pl.pallas_call(
        functools.partial(atm_kernel, plan),
        name="atmosphere",
        grid_spec=pltpu.PrefetchScalarGridSpec(
            num_scalar_prefetch=4,
            grid=(inner // part,),
            in_specs=[
                whole((rows, width)),
                whole((1, width)),
                pl.BlockSpec((width, part), lambda i, *_: (0, i)),
                pl.BlockSpec((part, width), lambda i, *_: (i, 0)),
                whole(w_flux.shape),
                pl.BlockSpec(memory_space=pltpu.HBM),
            ],
            out_specs=[
                whole((rows, width)),
                whole((rows, features)),
                pl.BlockSpec(memory_space=pltpu.HBM),
            ],
            scratch_shapes=[
                pltpu.VMEM((rows, width), BF16),
                pltpu.VMEM((rows, width), F32),
                *remap_scratch(plan, entries, block, features),
            ],
        ),
        out_shape=[
            pltpu.HBM((rows, width), BF16),
            pltpu.HBM((rows, features), BF16),
            pltpu.HBM((peers, plan[3] * block + 16, features), BF16),
        ],
        compiler_params=pltpu.CompilerParams(vmem_limit_bytes=56 << 20),
    )(
        half,
        target,
        source,
        target_block,
        in_hbm(columns),
        in_hbm(gain[None, :]),
        in_hbm(w_up),
        in_hbm(w_down),
        in_hbm(w_flux),
        in_hbm(weights),
    )


def near_kernel(
    plan,
    half_ref,
    target_ref,
    source_ref,
    block_ref,
    surface_ref,
    weight_ref,
    near_ref,
    listed,
    slots,
    counts,
    weights,
    made,
    labels,
    tile,
    sems,
    tile_sem,
    weight_sem,
):
    fetch = pltpu.make_async_copy(weight_ref, weights, weight_sem)
    fetch.start()
    count = pick(plan, False, half_ref, target_ref, listed, slots, counts)
    fetch.wait()
    multiply(plan, count, source_ref, block_ref, surface_ref, weights, listed, slots, made, labels, tile, near_ref, sems, tile_sem)


def near_remap(plan, half, target, source, target_block, surface, weights):
    entries, block, _ = weights.shape
    features = surface.shape[1]
    peers = plan[0] * plan[2]
    return pl.pallas_call(
        functools.partial(near_kernel, plan),
        name="near_remap",
        grid_spec=pltpu.PrefetchScalarGridSpec(
            num_scalar_prefetch=4,
            grid=(1,),
            in_specs=[whole(surface.shape), pl.BlockSpec(memory_space=pltpu.HBM)],
            out_specs=pl.BlockSpec(memory_space=pltpu.HBM),
            scratch_shapes=remap_scratch(plan, entries, block, features),
        ),
        out_shape=pltpu.HBM((peers, plan[3] * block + 16, features), BF16),
        compiler_params=pltpu.CompilerParams(vmem_limit_bytes=48 << 20),
    )(half, target, source, target_block, in_hbm(surface), in_hbm(weights))


def merge_kernel(capacity, arrived_ref, out_ref, arrived, tile, listed, labels, total, sems, tile_sem):
    peers = arrived.shape[0]
    block = out_ref.shape[1]

    def fetch(peer):
        return pltpu.make_async_copy(
            arrived_ref.at[peer, pl.ds(0, capacity * block)], arrived.at[peer], sems.at[peer]
        )

    told = pltpu.make_async_copy(
        arrived_ref.at[:, pl.ds(capacity * block, tile.shape[1])], tile, tile_sem
    )
    told.start()
    for peer in range(peers):
        fetch(peer).start()
    total[...] = jnp.zeros_like(total)
    told.wait()
    listed[...] = jnp.max(tile[...].astype(F32), axis=1).astype(jnp.int32)
    read = pltpu.make_async_copy(listed, labels, tile_sem)
    read.start()
    read.wait()

    def add(peer, carry):
        fetch(peer).wait()
        for rank in range(capacity):
            label = labels[peer, rank]

            @pl.when(label >= 0)
            def _():
                total[label] += arrived[peer, rank * block : (rank + 1) * block].astype(F32)

        return carry

    lax.fori_loop(0, peers, add, 0)
    out_ref[...] = total[...].astype(BF16)


def merged(capacity, arrived, blocks, block):
    peers, _, features = arrived.shape
    return pl.pallas_call(
        functools.partial(merge_kernel, capacity),
        name="merge",
        grid=(1,),
        in_specs=[pl.BlockSpec(memory_space=pltpu.HBM)],
        out_specs=whole((blocks, block, features)),
        scratch_shapes=[
            pltpu.VMEM((peers, capacity * block, features), BF16),
            pltpu.VMEM((peers, 16, features), BF16),
            pltpu.VMEM((peers, features), jnp.int32),
            pltpu.SMEM((peers, features), jnp.int32),
            pltpu.VMEM((blocks, block, features), F32),
            pltpu.SemaphoreType.DMA((peers,)),
            pltpu.SemaphoreType.DMA,
        ],
        out_shape=jax.ShapeDtypeStruct((blocks, block, features), BF16),
        compiler_params=pltpu.CompilerParams(vmem_limit_bytes=32 << 20),
    )(in_hbm(arrived))


def ocean_kernel(mix_ref, near_ref, far_ref, now_ref, sea_ref, force_ref, gain_ref, up_ref, down_ref, out_ref):
    forcing = (near_ref[...].astype(F32) + far_ref[...].astype(F32)).astype(BF16)
    driven = mix_ref[...].astype(F32) + lax.dot_general(
        force_ref[...], forcing, (((1,), (1,)), ((), ())), preferred_element_type=F32
    )
    normed = (normalised(driven, 0) * gain_ref[...]).astype(BF16)
    hidden = gelu(jnp.dot(up_ref[...], normed, preferred_element_type=F32).astype(BF16))
    change = jnp.dot(down_ref[...], hidden, preferred_element_type=F32)
    out_ref[...] = (
        now_ref[...].astype(F32) + sea_ref[...].astype(F32) * change
    ).astype(BF16)


def ocean(mixing, near, far, now, sea, w_force, gain, w_up, w_down):
    channels, cells = now.shape
    features = near.shape[1]
    part = cells // 3
    if part % 128:
        part = cells
    tall = pl.BlockSpec((channels, part), lambda i: (0, i))
    flat = pl.BlockSpec((part, features), lambda i: (i, 0))
    return pl.pallas_call(
        ocean_kernel,
        name="ocean",
        grid=(cells // part,),
        in_specs=[
            tall,
            flat,
            flat,
            tall,
            pl.BlockSpec((1, part), lambda i: (0, i)),
            whole(w_force.shape),
            whole((channels, 1)),
            whole(w_up.shape),
            whole(w_down.shape),
        ],
        out_specs=tall,
        out_shape=jax.ShapeDtypeStruct((channels, cells), BF16),
        compiler_params=pltpu.CompilerParams(vmem_limit_bytes=32 << 20),
    )(
        in_vmem(mixing),
        in_vmem(near),
        in_vmem(far),
        in_vmem(now),
        in_vmem(sea[None, :]),
        in_vmem(w_force),
        in_vmem(gain[:, None]),
        in_vmem(w_up),
        in_vmem(w_down),
    )


def edge_rows(block):
    count = math.prod(lax.axis_size(axis) for axis in ALL)
    even = (lax.axis_index(ALL) & 1) == 0
    first, last = block[:, :OX], block[:, -OX:]

    def exchanged(mine, start):
        pairs = [(i, i + 1) for i in range(start, count - 1, 2)]
        return lax.ppermute(mine, ALL, pairs + [(upper, lower) for lower, upper in pairs])

    across = exchanged(jnp.where(even, first, last), 1)
    beside = exchanged(jnp.where(even, last, first), 0)
    return even, across, beside


def flat_mixing(padded_flat, kernel, row_len, cell_count):
    extended = jnp.pad(padded_flat.astype(F32), ((0, 0), (row_len, row_len)))
    column_at = (jnp.arange(cell_count, dtype=jnp.int32) % row_len)[None, :]
    first_col = column_at == 0
    last_col = column_at == row_len - 1

    def window(offset):
        return lax.slice_in_dim(extended, row_len + offset, row_len + offset + cell_count, axis=1)

    summed = jnp.zeros((padded_flat.shape[0], cell_count), F32)
    for row_step in range(3):
        base = row_step * row_len
        for col_step in range(3):
            if col_step == 0:
                shifted = jnp.where(first_col, window(base + row_len - 1), window(base - 1))
            elif col_step == 2:
                shifted = jnp.where(last_col, window(base - row_len + 1), window(base + 1))
            else:
                shifted = window(base)
            summed = summed + kernel[:, 3 * row_step + col_step][:, None] * shifted
    return summed


def local(
    atm_state,
    gain_atm,
    w_up_atm,
    w_down_atm,
    w_flux,
    ent_source,
    ent_target,
    ent_block,
    remap_weights,
    ocean_state,
    land_sea,
    conv_kernel,
    w_force,
    gain_ocn,
    w_up_ocn,
    w_down_ocn,
):
    sections, halves, nears = (lax.axis_size(axis) for axis in ALL)
    half = lax.axis_index("half")
    peers = sections * nears
    entries, block_rows, _ = remap_weights.shape
    capacity = max(2, 2 * entries // (peers * halves))
    cell_count = ocean_state.shape[1]
    ocean_blocks = cell_count // block_rows

    def exchange(values):
        return lax.all_to_all(values, PEERS, split_axis=0, concat_axis=0, tiled=True)

    plan = (sections, halves, nears, capacity)
    entry = (half[None], ent_target[:, 0], ent_source, ent_block)
    atm_next, surface, far_made = atmosphere(
        plan, *entry, atm_state, gain_atm, w_up_atm, w_down_atm, w_flux, remap_weights
    )
    even, across, beside = edge_rows(ocean_state)
    far_made, across, beside = lax.optimization_barrier((far_made, across, beside))
    far_arrived = exchange(far_made)
    near_made = near_remap(plan, *entry, surface, remap_weights)
    low, high = jnp.where(even, across, beside), jnp.where(even, beside, across)
    padded = jnp.concatenate([low, ocean_state, high], axis=1)
    mixing = flat_mixing(padded, conv_kernel, OX, cell_count).astype(BF16)
    far_arrived, near_made, mixing = lax.optimization_barrier((far_arrived, near_made, mixing))
    near_arrived = exchange(near_made)
    far_sum = merged(capacity, far_arrived, ocean_blocks, block_rows)
    far_sum = lax.ppermute(far_sum, "half", [(0, 1), (1, 0)])
    near_sum = merged(capacity, near_arrived, ocean_blocks, block_rows)
    features = far_sum.shape[2]
    ocean_next = ocean(
        mixing,
        near_sum.reshape(cell_count, features),
        far_sum.reshape(cell_count, features),
        ocean_state,
        land_sea,
        w_force.T,
        gain_ocn,
        w_up_ocn.T,
        w_down_ocn.T,
    )
    return (atm_next, ocean_next)


def solution(mesh):
    sections, tiles = mesh.shape["sec"], mesh.shape["tile"]
    fine = Mesh(mesh.devices.reshape(sections, 2, tiles // 2), ALL)
    placed = (
        P(ALL, None),
        P(),
        P(),
        P(),
        P(),
        P(ALL),
        P(ALL, None),
        P(ALL),
        P(ALL, None, None),
        P(None, ALL),
        P(ALL),
        P(),
        P(),
        P(),
        P(),
        P(),
    )
    return jax.shard_map(
        local,
        mesh=fine,
        in_specs=placed,
        out_specs=(P(ALL, None), P(None, ALL)),
        check_vma=False,
    )
```

```python
import functools
import math

import jax
import jax.numpy as jnp
from jax import lax
from jax.experimental import pallas as pl
from jax.experimental.pallas import tpu as pltpu
from jax.sharding import Mesh, PartitionSpec as P

OX = 1440
ALL = ("sec", "half", "near")
PEERS = ("sec", "near")
F32 = jnp.float32
BF16 = jnp.bfloat16


def gelu(x):
    half = 0.5 * x
    return half + half * jnp.tanh(x * (0.7978845608028654 + 0.035677408136300125 * (x * x)))


def normalised(values, axis):
    centred = values - jnp.mean(values, axis=axis, keepdims=True)
    spread_sq = jnp.mean(centred * centred, axis=axis, keepdims=True)
    return centred * lax.rsqrt(spread_sq + 1e-05)


def in_hbm(value):
    return pltpu.with_memory_space_constraint(value, pltpu.HBM)


def in_vmem(value):
    return pltpu.with_memory_space_constraint(value, pltpu.VMEM)


def whole(shape):
    return pl.BlockSpec(shape, lambda *_: (0,) * len(shape))


def split(index, size):
    if size & (size - 1) == 0:
        return index >> (size.bit_length() - 1), index & (size - 1)
    return lax.div(index, size), lax.rem(index, size)


def pick(plan, want_far, half_ref, target_ref, listed, slots, counts):
    _, halves, nears, capacity = plan

    def none(tile, carry):
        counts[tile] = 0
        return carry

    def step(entry, count):
        target = target_ref[entry]
        rank = counts[target]
        counts[target] = rank + 1
        upper, near = split(target, nears)
        sec, half = split(upper, halves)
        listed[count] = entry
        slots[count] = (sec * nears + near) * capacity + rank
        far = (half != half_ref[0]).astype(jnp.int32)
        return count + (far if want_far else 1 - far)

    lax.fori_loop(0, counts.shape[0], none, 0)
    return lax.fori_loop(0, target_ref.shape[0], step, jnp.int32(0), unroll=4)


def multiply(plan, count, source_ref, block_ref, surface_ref, weights, listed, slots, made, labels, tile, out_ref, sems, tile_sem):
    capacity = plan[3]
    block = weights.shape[1]
    labels[...] = jnp.full_like(labels, -1)
    lane = lax.broadcasted_iota(jnp.int32, (1, labels.shape[1]), 1)

    def copy(at):
        peer, rank = split(slots[at], capacity)
        rows = pl.ds(pl.multiple_of(rank * block, block), block)
        return pltpu.make_async_copy(made.at[at], out_ref.at[peer, rows], sems.at[at])

    def group(size, first):
        for i in range(size):
            entry = listed[first + i]
            rows = pl.ds(pl.multiple_of(source_ref[entry] * block, block), block)
            made[first + i] = jnp.dot(
                weights[entry], surface_ref[rows, :], preferred_element_type=F32
            ).astype(BF16)
            peer, rank = split(slots[first + i], capacity)
            row = labels[pl.ds(peer, 1), :]
            labels[pl.ds(peer, 1), :] = jnp.where(lane == rank, block_ref[entry], row)
        for i in range(size):
            copy(first + i).start()

    def eight(i, carry):
        group(8, i * 8)
        return carry

    def one(i, carry):
        group(1, i)
        return carry

    def drain(i, carry):
        copy(i).wait()
        return carry

    full = count >> 3
    lax.fori_loop(0, full, eight, 0)
    lax.fori_loop(full * 8, count, one, 0)
    tile[...] = jnp.broadcast_to(labels[...].astype(F32)[:, None, :], tile.shape).astype(BF16)
    told = pltpu.make_async_copy(
        tile, out_ref.at[:, pl.ds(capacity * block, tile.shape[1])], tile_sem
    )
    told.start()
    lax.fori_loop(0, count, drain, 0)
    told.wait()


def remap_scratch(plan, entries, block, features):
    sections, halves, nears, _ = plan
    peers = sections * nears
    return [
        pltpu.SMEM((entries + 1,), jnp.int32),
        pltpu.SMEM((entries + 1,), jnp.int32),
        pltpu.SMEM((sections * halves * nears,), jnp.int32),
        pltpu.VMEM((entries, block, block), BF16),
        pltpu.VMEM((entries, block, features), BF16),
        pltpu.VMEM((peers, 128), jnp.int32),
        pltpu.VMEM((peers, 16, features), BF16),
        pltpu.SemaphoreType.DMA((entries,)),
        pltpu.SemaphoreType.DMA,
        pltpu.SemaphoreType.DMA,
    ]


def atm_kernel(
    plan,
    half_ref,
    target_ref,
    source_ref,
    block_ref,
    x_ref,
    gain_ref,
    up_ref,
    down_ref,
    flux_ref,
    weight_ref,
    next_ref,
    surface_ref,
    far_ref,
    normed,
    total,
    listed,
    slots,
    counts,
    weights,
    made,
    labels,
    tile,
    sems,
    tile_sem,
    weight_sem,
):
    step = pl.program_id(0)
    last = step == pl.num_programs(0) - 1
    parts = [slice(at, at + x_ref.shape[0] // 2) for at in (0, x_ref.shape[0] // 2)]
    fetch = pltpu.make_async_copy(weight_ref, weights, weight_sem)

    @pl.when(step == 0)
    def _():
        for rows in parts:
            values = x_ref[rows, :].astype(F32)
            normed[rows, :] = (normalised(values, -1) * gain_ref[...]).astype(BF16)
            total[rows, :] = values

    @pl.when(step == 1)
    def _():
        fetch.start()

    for rows in parts:
        raised = jnp.dot(normed[rows, :], up_ref[...], preferred_element_type=F32)
        hidden = gelu(raised.astype(BF16))
        total[rows, :] += jnp.dot(hidden, down_ref[...], preferred_element_type=F32)

    @pl.when(last)
    def _():
        for rows in parts:
            updated = total[rows, :].astype(BF16)
            next_ref[rows, :] = updated
            surface_ref[rows, :] = jnp.dot(
                updated, flux_ref[...], preferred_element_type=F32
            ).astype(BF16)
        count = pick(plan, True, half_ref, target_ref, listed, slots, counts)
        fetch.wait()
        multiply(plan, count, source_ref, block_ref, surface_ref, weights, listed, slots, made, labels, tile, far_ref, sems, tile_sem)


def atmosphere(plan, half, target, source, target_block, columns, gain, w_up, w_down, w_flux, weights):
    rows, width = columns.shape
    features = w_flux.shape[1]
    inner = w_up.shape[1]
    entries, block, _ = weights.shape
    part = inner // 4
    peers = plan[0] * plan[2]
    return pl.pallas_call(
        functools.partial(atm_kernel, plan),
        name="atmosphere",
        grid_spec=pltpu.PrefetchScalarGridSpec(
            num_scalar_prefetch=4,
            grid=(inner // part,),
            in_specs=[
                whole((rows, width)),
                whole((1, width)),
                pl.BlockSpec((width, part), lambda i, *_: (0, i)),
                pl.BlockSpec((part, width), lambda i, *_: (i, 0)),
                whole(w_flux.shape),
                pl.BlockSpec(memory_space=pltpu.HBM),
            ],
            out_specs=[
                whole((rows, width)),
                whole((rows, features)),
                pl.BlockSpec(memory_space=pltpu.HBM),
            ],
            scratch_shapes=[
                pltpu.VMEM((rows, width), BF16),
                pltpu.VMEM((rows, width), F32),
                *remap_scratch(plan, entries, block, features),
            ],
        ),
        out_shape=[
            pltpu.HBM((rows, width), BF16),
            pltpu.HBM((rows, features), BF16),
            pltpu.HBM((peers, plan[3] * block + 16, features), BF16),
        ],
        compiler_params=pltpu.CompilerParams(vmem_limit_bytes=56 << 20),
    )(
        half,
        target,
        source,
        target_block,
        in_hbm(columns),
        in_hbm(gain[None, :]),
        in_hbm(w_up),
        in_hbm(w_down),
        in_hbm(w_flux),
        in_hbm(weights),
    )


def near_kernel(
    plan,
    half_ref,
    target_ref,
    source_ref,
    block_ref,
    surface_ref,
    weight_ref,
    near_ref,
    listed,
    slots,
    counts,
    weights,
    made,
    labels,
    tile,
    sems,
    tile_sem,
    weight_sem,
):
    fetch = pltpu.make_async_copy(weight_ref, weights, weight_sem)
    fetch.start()
    count = pick(plan, False, half_ref, target_ref, listed, slots, counts)
    fetch.wait()
    multiply(plan, count, source_ref, block_ref, surface_ref, weights, listed, slots, made, labels, tile, near_ref, sems, tile_sem)


def near_remap(plan, half, target, source, target_block, surface, weights):
    entries, block, _ = weights.shape
    features = surface.shape[1]
    peers = plan[0] * plan[2]
    return pl.pallas_call(
        functools.partial(near_kernel, plan),
        name="near_remap",
        grid_spec=pltpu.PrefetchScalarGridSpec(
            num_scalar_prefetch=4,
            grid=(1,),
            in_specs=[whole(surface.shape), pl.BlockSpec(memory_space=pltpu.HBM)],
            out_specs=pl.BlockSpec(memory_space=pltpu.HBM),
            scratch_shapes=remap_scratch(plan, entries, block, features),
        ),
        out_shape=pltpu.HBM((peers, plan[3] * block + 16, features), BF16),
        compiler_params=pltpu.CompilerParams(vmem_limit_bytes=48 << 20),
    )(half, target, source, target_block, in_hbm(surface), in_hbm(weights))


def merge_kernel(capacity, arrived_ref, out_ref, arrived, tile, listed, labels, total, sems, tile_sem):
    peers = arrived.shape[0]
    block = out_ref.shape[1]

    def fetch(peer):
        return pltpu.make_async_copy(
            arrived_ref.at[peer, pl.ds(0, capacity * block)], arrived.at[peer], sems.at[peer]
        )

    told = pltpu.make_async_copy(
        arrived_ref.at[:, pl.ds(capacity * block, tile.shape[1])], tile, tile_sem
    )
    told.start()
    for peer in range(peers):
        fetch(peer).start()
    total[...] = jnp.zeros_like(total)
    told.wait()
    listed[...] = jnp.max(tile[...].astype(F32), axis=1).astype(jnp.int32)
    read = pltpu.make_async_copy(listed, labels, tile_sem)
    read.start()
    read.wait()

    def add(peer, carry):
        fetch(peer).wait()
        for rank in range(capacity):
            label = labels[peer, rank]

            @pl.when(label >= 0)
            def _():
                total[label] += arrived[peer, rank * block : (rank + 1) * block].astype(F32)

        return carry

    lax.fori_loop(0, peers, add, 0)
    out_ref[...] = total[...].astype(BF16)


def merged(capacity, arrived, blocks, block):
    peers, _, features = arrived.shape
    return pl.pallas_call(
        functools.partial(merge_kernel, capacity),
        name="merge",
        grid=(1,),
        in_specs=[pl.BlockSpec(memory_space=pltpu.HBM)],
        out_specs=whole((blocks, block, features)),
        scratch_shapes=[
            pltpu.VMEM((peers, capacity * block, features), BF16),
            pltpu.VMEM((peers, 16, features), BF16),
            pltpu.VMEM((peers, features), jnp.int32),
            pltpu.SMEM((peers, features), jnp.int32),
            pltpu.VMEM((blocks, block, features), F32),
            pltpu.SemaphoreType.DMA((peers,)),
            pltpu.SemaphoreType.DMA,
        ],
        out_shape=jax.ShapeDtypeStruct((blocks, block, features), BF16),
        compiler_params=pltpu.CompilerParams(vmem_limit_bytes=32 << 20),
    )(in_hbm(arrived))


def ocean_kernel(mix_ref, near_ref, far_ref, now_ref, sea_ref, force_ref, gain_ref, up_ref, down_ref, out_ref):
    forcing = (near_ref[...].astype(F32) + far_ref[...].astype(F32)).astype(BF16)
    driven = mix_ref[...].astype(F32) + lax.dot_general(
        force_ref[...], forcing, (((1,), (1,)), ((), ())), preferred_element_type=F32
    )
    normed = (normalised(driven, 0) * gain_ref[...]).astype(BF16)
    hidden = gelu(jnp.dot(up_ref[...], normed, preferred_element_type=F32).astype(BF16))
    change = jnp.dot(down_ref[...], hidden, preferred_element_type=F32)
    out_ref[...] = (
        now_ref[...].astype(F32) + sea_ref[...].astype(F32) * change
    ).astype(BF16)


def ocean(mixing, near, far, now, sea, w_force, gain, w_up, w_down):
    channels, cells = now.shape
    features = near.shape[1]
    part = cells // 3
    if part % 128:
        part = cells
    tall = pl.BlockSpec((channels, part), lambda i: (0, i))
    flat = pl.BlockSpec((part, features), lambda i: (i, 0))
    return pl.pallas_call(
        ocean_kernel,
        name="ocean",
        grid=(cells // part,),
        in_specs=[
            tall,
            flat,
            flat,
            tall,
            pl.BlockSpec((1, part), lambda i: (0, i)),
            whole(w_force.shape),
            whole((channels, 1)),
            whole(w_up.shape),
            whole(w_down.shape),
        ],
        out_specs=tall,
        out_shape=jax.ShapeDtypeStruct((channels, cells), BF16),
        compiler_params=pltpu.CompilerParams(vmem_limit_bytes=32 << 20),
    )(
        in_vmem(mixing),
        in_vmem(near),
        in_vmem(far),
        in_vmem(now),
        in_vmem(sea[None, :]),
        in_vmem(w_force),
        in_vmem(gain),
        in_vmem(w_up),
        in_vmem(w_down),
    )


def exchanged(row, start):
    count = math.prod(lax.axis_size(axis) for axis in ALL)
    pairs = [(i, i + 1) for i in range(start, count - 1, 2)]
    return lax.ppermute(row, ALL, pairs + [(upper, lower) for lower, upper in pairs])


def row_mixing(row, taps):
    row = row.astype(F32)
    return sum(taps[:, step : step + 1] * jnp.roll(row, 1 - step, axis=1) for step in range(3))


def flat_mixing(padded_flat, kernel, row_len, cell_count):
    extended = jnp.pad(padded_flat.astype(F32), ((0, 0), (row_len, row_len)))
    column_at = (jnp.arange(cell_count, dtype=jnp.int32) % row_len)[None, :]
    first_col = column_at == 0
    last_col = column_at == row_len - 1

    def window(offset):
        return lax.slice_in_dim(extended, row_len + offset, row_len + offset + cell_count, axis=1)

    summed = jnp.zeros((padded_flat.shape[0], cell_count), F32)
    for row_step in range(3):
        base = row_step * row_len
        for col_step in range(3):
            if col_step == 0:
                shifted = jnp.where(first_col, window(base + row_len - 1), window(base - 1))
            elif col_step == 2:
                shifted = jnp.where(last_col, window(base - row_len + 1), window(base + 1))
            else:
                shifted = window(base)
            summed = summed + kernel[:, 3 * row_step + col_step][:, None] * shifted
    return summed


def local(
    atm_state,
    gain_atm,
    w_up_atm,
    w_down_atm,
    w_flux,
    ent_source,
    ent_target,
    ent_block,
    remap_weights,
    ocean_state,
    land_sea,
    conv_kernel,
    w_force,
    gain_ocn,
    w_up_ocn,
    w_down_ocn,
):
    sections, halves, nears = (lax.axis_size(axis) for axis in ALL)
    half = lax.axis_index("half")
    peers = sections * nears
    entries, block_rows, _ = remap_weights.shape
    capacity = max(2, 2 * entries // (peers * halves))
    cell_count = ocean_state.shape[1]
    ocean_blocks = cell_count // block_rows

    def exchange(values):
        return lax.all_to_all(values, PEERS, split_axis=0, concat_axis=0, tiled=True)

    plan = (sections, halves, nears, capacity)
    entry = (half[None], ent_target[:, 0], ent_source, ent_block)
    atm_next, surface, far_made = atmosphere(
        plan, *entry, atm_state, gain_atm, w_up_atm, w_down_atm, w_flux, remap_weights
    )
    even = (lax.axis_index(ALL) & 1) == 0
    first, last = ocean_state[:, :OX], ocean_state[:, -OX:]
    across = exchanged(jnp.where(even, first, last), 1)
    far_made, across = lax.optimization_barrier((far_made, across))
    far_arrived = exchange(far_made)
    near_made = near_remap(plan, *entry, surface, remap_weights)
    none = jnp.zeros_like(across)
    low, high = jnp.where(even, across, none), jnp.where(even, none, across)
    padded = jnp.concatenate([low, ocean_state, high], axis=1)
    mixing = flat_mixing(padded, conv_kernel, OX, cell_count)
    beside = jnp.where(even, last, first)
    taps = jnp.where(even, conv_kernel[:, 6:9], conv_kernel[:, 0:3])
    ocean_weights = (w_force.T, gain_ocn[:, None], w_up_ocn.T, w_down_ocn.T)
    far_arrived, near_made, mixing, beside, taps, ocean_weights = lax.optimization_barrier(
        (far_arrived, near_made, mixing, beside, taps, ocean_weights)
    )
    near_arrived = exchange(near_made)
    beside = exchanged(beside, 0)
    far_sum = merged(capacity, far_arrived, ocean_blocks, block_rows)
    far_sum = lax.ppermute(far_sum, "half", [(0, 1), (1, 0)])
    added = row_mixing(beside, taps)
    rest = cell_count - OX
    mixing = (
        mixing
        + jnp.pad(jnp.where(even, 0.0, added), ((0, 0), (0, rest)))
        + jnp.pad(jnp.where(even, added, 0.0), ((0, 0), (rest, 0)))
    ).astype(BF16)
    near_arrived, mixing = lax.optimization_barrier((near_arrived, mixing))
    near_sum = merged(capacity, near_arrived, ocean_blocks, block_rows)
    features = far_sum.shape[2]
    ocean_next = ocean(
        mixing,
        near_sum.reshape(cell_count, features),
        far_sum.reshape(cell_count, features),
        ocean_state,
        land_sea,
        *ocean_weights,
    )
    return (atm_next, ocean_next)


def solution(mesh):
    sections, tiles = mesh.shape["sec"], mesh.shape["tile"]
    fine = Mesh(mesh.devices.reshape(sections, 2, tiles // 2), ALL)
    placed = (
        P(ALL, None),
        P(),
        P(),
        P(),
        P(),
        P(ALL),
        P(ALL, None),
        P(ALL),
        P(ALL, None, None),
        P(None, ALL),
        P(ALL),
        P(),
        P(),
        P(),
        P(),
        P(),
    )
    return jax.shard_map(
        local,
        mesh=fine,
        in_specs=placed,
        out_specs=(P(ALL, None), P(None, ALL)),
        check_vma=False,
    )
```

```python
import functools
import math

import jax
import jax.numpy as jnp
from jax import lax
from jax.experimental import pallas as pl
from jax.experimental.pallas import tpu as pltpu
from jax.sharding import Mesh, PartitionSpec as P

OX = 1440
ALL = ("sec", "half", "near")
PEERS = ("sec", "near")
F32 = jnp.float32
BF16 = jnp.bfloat16


def gelu(x):
    half = 0.5 * x
    return half + half * jnp.tanh(x * (0.7978845608028654 + 0.035677408136300125 * (x * x)))


def normalised(values, axis):
    centred = values - jnp.mean(values, axis=axis, keepdims=True)
    spread_sq = jnp.mean(centred * centred, axis=axis, keepdims=True)
    return centred * lax.rsqrt(spread_sq + 1e-05)


def in_hbm(value):
    return pltpu.with_memory_space_constraint(value, pltpu.HBM)


def in_vmem(value):
    return pltpu.with_memory_space_constraint(value, pltpu.VMEM)


def whole(shape):
    return pl.BlockSpec(shape, lambda *_: (0,) * len(shape))


def split(index, size):
    if size & (size - 1) == 0:
        return index >> (size.bit_length() - 1), index & (size - 1)
    return lax.div(index, size), lax.rem(index, size)


def pick(plan, want_far, half_ref, target_ref, listed, slots, counts):
    _, halves, nears, capacity = plan

    def none(tile, carry):
        counts[tile] = 0
        return carry

    def step(entry, count):
        target = target_ref[entry]
        rank = counts[target]
        counts[target] = rank + 1
        upper, near = split(target, nears)
        sec, half = split(upper, halves)
        listed[count] = entry
        slots[count] = (sec * nears + near) * capacity + rank
        far = (half != half_ref[0]).astype(jnp.int32)
        return count + (far if want_far else 1 - far)

    lax.fori_loop(0, counts.shape[0], none, 0)
    return lax.fori_loop(0, target_ref.shape[0], step, jnp.int32(0), unroll=4)


def multiply(plan, count, source_ref, block_ref, surface_ref, weights, listed, slots, made, labels, tile, out_ref, sems, tile_sem):
    capacity = plan[3]
    block = weights.shape[1]
    labels[...] = jnp.full_like(labels, -1)
    lane = lax.broadcasted_iota(jnp.int32, (1, labels.shape[1]), 1)

    def copy(at):
        peer, rank = split(slots[at], capacity)
        rows = pl.ds(pl.multiple_of(rank * block, block), block)
        return pltpu.make_async_copy(made.at[at], out_ref.at[peer, rows], sems.at[at])

    def group(size, first):
        for i in range(size):
            entry = listed[first + i]
            rows = pl.ds(pl.multiple_of(source_ref[entry] * block, block), block)
            made[first + i] = jnp.dot(
                weights[entry], surface_ref[rows, :], preferred_element_type=F32
            ).astype(BF16)
            peer, rank = split(slots[first + i], capacity)
            row = labels[pl.ds(peer, 1), :]
            labels[pl.ds(peer, 1), :] = jnp.where(lane == rank, block_ref[entry], row)
        for i in range(size):
            copy(first + i).start()

    def eight(i, carry):
        group(8, i * 8)
        return carry

    def one(i, carry):
        group(1, i)
        return carry

    def drain(i, carry):
        copy(i).wait()
        return carry

    full = count >> 3
    lax.fori_loop(0, full, eight, 0)
    lax.fori_loop(full * 8, count, one, 0)
    tile[...] = jnp.broadcast_to(labels[...].astype(F32)[:, None, :], tile.shape).astype(BF16)
    told = pltpu.make_async_copy(
        tile, out_ref.at[:, pl.ds(capacity * block, tile.shape[1])], tile_sem
    )
    told.start()
    lax.fori_loop(0, count, drain, 0)
    told.wait()


def remap_scratch(plan, entries, block, features):
    sections, halves, nears, _ = plan
    peers = sections * nears
    return [
        pltpu.SMEM((entries + 1,), jnp.int32),
        pltpu.SMEM((entries + 1,), jnp.int32),
        pltpu.SMEM((sections * halves * nears,), jnp.int32),
        pltpu.VMEM((entries, block, block), BF16),
        pltpu.VMEM((entries, block, features), BF16),
        pltpu.VMEM((peers, 128), jnp.int32),
        pltpu.VMEM((peers, 16, features), BF16),
        pltpu.SemaphoreType.DMA((entries,)),
        pltpu.SemaphoreType.DMA,
        pltpu.SemaphoreType.DMA,
    ]


def atm_kernel(
    plan,
    half_ref,
    target_ref,
    source_ref,
    block_ref,
    x_ref,
    gain_ref,
    up_ref,
    down_ref,
    flux_ref,
    weight_ref,
    next_ref,
    surface_ref,
    far_ref,
    normed,
    total,
    listed,
    slots,
    counts,
    weights,
    made,
    labels,
    tile,
    sems,
    tile_sem,
    weight_sem,
):
    step = pl.program_id(0)
    last = step == pl.num_programs(0) - 1
    parts = [slice(at, at + x_ref.shape[0] // 2) for at in (0, x_ref.shape[0] // 2)]
    fetch = pltpu.make_async_copy(weight_ref, weights, weight_sem)

    @pl.when(step == 0)
    def _():
        for rows in parts:
            values = x_ref[rows, :].astype(F32)
            normed[rows, :] = (normalised(values, -1) * gain_ref[...]).astype(BF16)
            total[rows, :] = values

    @pl.when(step == 1)
    def _():
        fetch.start()

    for rows in parts:
        raised = jnp.dot(normed[rows, :], up_ref[...], preferred_element_type=F32)
        hidden = gelu(raised.astype(BF16))
        total[rows, :] += jnp.dot(hidden, down_ref[...], preferred_element_type=F32)

    @pl.when(last)
    def _():
        for rows in parts:
            updated = total[rows, :].astype(BF16)
            next_ref[rows, :] = updated
            surface_ref[rows, :] = jnp.dot(
                updated, flux_ref[...], preferred_element_type=F32
            ).astype(BF16)
        count = pick(plan, True, half_ref, target_ref, listed, slots, counts)
        fetch.wait()
        multiply(plan, count, source_ref, block_ref, surface_ref, weights, listed, slots, made, labels, tile, far_ref, sems, tile_sem)


def atmosphere(plan, half, target, source, target_block, columns, gain, w_up, w_down, w_flux, weights):
    rows, width = columns.shape
    features = w_flux.shape[1]
    inner = w_up.shape[1]
    entries, block, _ = weights.shape
    part = inner // 4
    peers = plan[0] * plan[2]
    return pl.pallas_call(
        functools.partial(atm_kernel, plan),
        name="atmosphere",
        grid_spec=pltpu.PrefetchScalarGridSpec(
            num_scalar_prefetch=4,
            grid=(inner // part,),
            in_specs=[
                whole((rows, width)),
                whole((1, width)),
                pl.BlockSpec((width, part), lambda i, *_: (0, i)),
                pl.BlockSpec((part, width), lambda i, *_: (i, 0)),
                whole(w_flux.shape),
                pl.BlockSpec(memory_space=pltpu.HBM),
            ],
            out_specs=[
                whole((rows, width)),
                whole((rows, features)),
                pl.BlockSpec(memory_space=pltpu.HBM),
            ],
            scratch_shapes=[
                pltpu.VMEM((rows, width), BF16),
                pltpu.VMEM((rows, width), F32),
                *remap_scratch(plan, entries, block, features),
            ],
        ),
        out_shape=[
            pltpu.HBM((rows, width), BF16),
            pltpu.HBM((rows, features), BF16),
            pltpu.HBM((peers, plan[3] * block + 16, features), BF16),
        ],
        compiler_params=pltpu.CompilerParams(vmem_limit_bytes=56 << 20),
    )(
        half,
        target,
        source,
        target_block,
        in_hbm(columns),
        in_hbm(gain[None, :]),
        in_hbm(w_up),
        in_hbm(w_down),
        in_hbm(w_flux),
        in_hbm(weights),
    )


def near_kernel(
    plan,
    half_ref,
    target_ref,
    source_ref,
    block_ref,
    surface_ref,
    weight_ref,
    near_ref,
    listed,
    slots,
    counts,
    weights,
    made,
    labels,
    tile,
    sems,
    tile_sem,
    weight_sem,
):
    fetch = pltpu.make_async_copy(weight_ref, weights, weight_sem)
    fetch.start()
    count = pick(plan, False, half_ref, target_ref, listed, slots, counts)
    fetch.wait()
    multiply(plan, count, source_ref, block_ref, surface_ref, weights, listed, slots, made, labels, tile, near_ref, sems, tile_sem)


def near_remap(plan, half, target, source, target_block, surface, weights):
    entries, block, _ = weights.shape
    features = surface.shape[1]
    peers = plan[0] * plan[2]
    return pl.pallas_call(
        functools.partial(near_kernel, plan),
        name="near_remap",
        grid_spec=pltpu.PrefetchScalarGridSpec(
            num_scalar_prefetch=4,
            grid=(1,),
            in_specs=[whole(surface.shape), pl.BlockSpec(memory_space=pltpu.HBM)],
            out_specs=pl.BlockSpec(memory_space=pltpu.HBM),
            scratch_shapes=remap_scratch(plan, entries, block, features),
        ),
        out_shape=pltpu.HBM((peers, plan[3] * block + 16, features), BF16),
        compiler_params=pltpu.CompilerParams(vmem_limit_bytes=48 << 20),
    )(half, target, source, target_block, in_hbm(surface), in_hbm(weights))


def merge_kernel(capacity, arrived_ref, out_ref, arrived, tile, listed, labels, total, sems, tile_sem):
    peers = arrived.shape[0]
    block = out_ref.shape[1]

    def fetch(peer):
        return pltpu.make_async_copy(
            arrived_ref.at[peer, pl.ds(0, capacity * block)], arrived.at[peer], sems.at[peer]
        )

    told = pltpu.make_async_copy(
        arrived_ref.at[:, pl.ds(capacity * block, tile.shape[1])], tile, tile_sem
    )
    told.start()
    for peer in range(peers):
        fetch(peer).start()
    total[...] = jnp.zeros_like(total)
    told.wait()
    listed[...] = jnp.max(tile[...].astype(F32), axis=1).astype(jnp.int32)
    read = pltpu.make_async_copy(listed, labels, tile_sem)
    read.start()
    read.wait()

    def add(peer, carry):
        fetch(peer).wait()
        for rank in range(capacity):
            label = labels[peer, rank]

            @pl.when(label >= 0)
            def _():
                total[label] += arrived[peer, rank * block : (rank + 1) * block].astype(F32)

        return carry

    lax.fori_loop(0, peers, add, 0)
    out_ref[...] = total[...].astype(BF16)


def merged(capacity, arrived, blocks, block):
    peers, _, features = arrived.shape
    return pl.pallas_call(
        functools.partial(merge_kernel, capacity),
        name="merge",
        grid=(1,),
        in_specs=[pl.BlockSpec(memory_space=pltpu.HBM)],
        out_specs=whole((blocks, block, features)),
        scratch_shapes=[
            pltpu.VMEM((peers, capacity * block, features), BF16),
            pltpu.VMEM((peers, 16, features), BF16),
            pltpu.VMEM((peers, features), jnp.int32),
            pltpu.SMEM((peers, features), jnp.int32),
            pltpu.VMEM((blocks, block, features), F32),
            pltpu.SemaphoreType.DMA((peers,)),
            pltpu.SemaphoreType.DMA,
        ],
        out_shape=jax.ShapeDtypeStruct((blocks, block, features), BF16),
        compiler_params=pltpu.CompilerParams(vmem_limit_bytes=32 << 20),
    )(in_hbm(arrived))


def ocean_kernel(mix_ref, near_ref, far_ref, now_ref, sea_ref, force_ref, gain_ref, up_ref, down_ref, out_ref):
    forcing = (near_ref[...].astype(F32) + far_ref[...].astype(F32)).astype(BF16)
    driven = mix_ref[...].astype(F32) + lax.dot_general(
        force_ref[...], forcing, (((1,), (1,)), ((), ())), preferred_element_type=F32
    )
    normed = (normalised(driven, 0) * gain_ref[...]).astype(BF16)
    hidden = gelu(jnp.dot(up_ref[...], normed, preferred_element_type=F32).astype(BF16))
    change = jnp.dot(down_ref[...], hidden, preferred_element_type=F32)
    out_ref[...] = (
        now_ref[...].astype(F32) + sea_ref[...].astype(F32) * change
    ).astype(BF16)


def ocean(mixing, near, far, now, sea, w_force, gain, w_up, w_down):
    channels, cells = now.shape
    features = near.shape[1]
    part = cells // 3
    if part % 128:
        part = cells
    tall = pl.BlockSpec((channels, part), lambda i: (0, i))
    flat = pl.BlockSpec((part, features), lambda i: (i, 0))
    return pl.pallas_call(
        ocean_kernel,
        name="ocean",
        grid=(cells // part,),
        in_specs=[
            tall,
            flat,
            flat,
            tall,
            pl.BlockSpec((1, part), lambda i: (0, i)),
            whole(w_force.shape),
            whole((channels, 1)),
            whole(w_up.shape),
            whole(w_down.shape),
        ],
        out_specs=tall,
        out_shape=jax.ShapeDtypeStruct((channels, cells), BF16),
        compiler_params=pltpu.CompilerParams(vmem_limit_bytes=32 << 20),
    )(
        in_vmem(mixing),
        in_vmem(near),
        in_vmem(far),
        in_vmem(now),
        in_vmem(sea[None, :]),
        in_vmem(w_force),
        in_vmem(gain),
        in_vmem(w_up),
        in_vmem(w_down),
    )


def exchanged(row, start):
    count = math.prod(lax.axis_size(axis) for axis in ALL)
    pairs = [(i, i + 1) for i in range(start, count - 1, 2)]
    return lax.ppermute(row, ALL, pairs + [(upper, lower) for lower, upper in pairs])


def row_mixing(row, taps):
    row = row.astype(F32)
    return sum(taps[:, step : step + 1] * jnp.roll(row, 1 - step, axis=1) for step in range(3))


def flat_mixing(padded_flat, kernel, row_len, cell_count):
    extended = jnp.pad(padded_flat.astype(F32), ((0, 0), (row_len, row_len)))
    column_at = (jnp.arange(cell_count, dtype=jnp.int32) % row_len)[None, :]
    first_col = column_at == 0
    last_col = column_at == row_len - 1

    def window(offset):
        return lax.slice_in_dim(extended, row_len + offset, row_len + offset + cell_count, axis=1)

    summed = jnp.zeros((padded_flat.shape[0], cell_count), F32)
    for row_step in range(3):
        base = row_step * row_len
        for col_step in range(3):
            if col_step == 0:
                shifted = jnp.where(first_col, window(base + row_len - 1), window(base - 1))
            elif col_step == 2:
                shifted = jnp.where(last_col, window(base - row_len + 1), window(base + 1))
            else:
                shifted = window(base)
            summed = summed + kernel[:, 3 * row_step + col_step][:, None] * shifted
    return summed


def local(
    atm_state,
    gain_atm,
    w_up_atm,
    w_down_atm,
    w_flux,
    ent_source,
    ent_target,
    ent_block,
    remap_weights,
    ocean_state,
    land_sea,
    conv_kernel,
    w_force,
    gain_ocn,
    w_up_ocn,
    w_down_ocn,
):
    sections, halves, nears = (lax.axis_size(axis) for axis in ALL)
    half = lax.axis_index("half")
    peers = sections * nears
    entries, block_rows, _ = remap_weights.shape
    capacity = max(2, 2 * entries // (peers * halves))
    cell_count = ocean_state.shape[1]
    ocean_blocks = cell_count // block_rows

    def exchange(values):
        return lax.all_to_all(values, PEERS, split_axis=0, concat_axis=0, tiled=True)

    plan = (sections, halves, nears, capacity)
    entry = (half[None], ent_target[:, 0], ent_source, ent_block)
    atm_next, surface, far_made = atmosphere(
        plan, *entry, atm_state, gain_atm, w_up_atm, w_down_atm, w_flux, remap_weights
    )
    even = (lax.axis_index(ALL) & 1) == 0
    first, last = ocean_state[:, :OX], ocean_state[:, -OX:]
    across = exchanged(jnp.where(even, first, last), 1)
    far_made, across, later_state = lax.optimization_barrier((far_made, across, ocean_state))
    far_arrived = exchange(far_made)
    near_made = near_remap(plan, *entry, surface, remap_weights)
    none = jnp.zeros_like(across)
    low, high = jnp.where(even, across, none), jnp.where(even, none, across)
    padded = jnp.concatenate([low, ocean_state, high], axis=1)
    mixing = flat_mixing(padded, conv_kernel, OX, cell_count)
    beside = jnp.where(even, later_state[:, -OX:], later_state[:, :OX])
    taps = jnp.where(even, conv_kernel[:, 6:9], conv_kernel[:, 0:3])
    ocean_weights = (w_force.T, gain_ocn[:, None], w_up_ocn.T, w_down_ocn.T)
    far_arrived, near_made, mixing, beside, taps, ocean_weights = lax.optimization_barrier(
        (far_arrived, near_made, mixing, beside, taps, ocean_weights)
    )
    near_arrived = exchange(near_made)
    beside = exchanged(beside, 0)
    far_sum = merged(capacity, far_arrived, ocean_blocks, block_rows)
    far_sum = lax.ppermute(far_sum, "half", [(0, 1), (1, 0)])
    added = row_mixing(beside, taps)
    rest = cell_count - OX
    mixing = (
        mixing
        + jnp.pad(jnp.where(even, 0.0, added), ((0, 0), (0, rest)))
        + jnp.pad(jnp.where(even, added, 0.0), ((0, 0), (rest, 0)))
    ).astype(BF16)
    near_arrived, mixing = lax.optimization_barrier((near_arrived, mixing))
    near_sum = merged(capacity, near_arrived, ocean_blocks, block_rows)
    features = far_sum.shape[2]
    ocean_next = ocean(
        mixing,
        near_sum.reshape(cell_count, features),
        far_sum.reshape(cell_count, features),
        ocean_state,
        land_sea,
        *ocean_weights,
    )
    return (atm_next, ocean_next)


def solution(mesh):
    sections, tiles = mesh.shape["sec"], mesh.shape["tile"]
    fine = Mesh(mesh.devices.reshape(sections, 2, tiles // 2), ALL)
    placed = (
        P(ALL, None),
        P(),
        P(),
        P(),
        P(),
        P(ALL),
        P(ALL, None),
        P(ALL),
        P(ALL, None, None),
        P(None, ALL),
        P(ALL),
        P(),
        P(),
        P(),
        P(),
        P(),
    )
    return jax.shard_map(
        local,
        mesh=fine,
        in_specs=placed,
        out_specs=(P(ALL, None), P(None, ALL)),
        check_vma=False,
    )
```

```python
import functools
import math

import jax
import jax.numpy as jnp
from jax import lax
from jax.experimental import pallas as pl
from jax.experimental.pallas import tpu as pltpu
from jax.sharding import Mesh, PartitionSpec as P

OX = 1440
ALL = ("sec", "half", "near")
PEERS = ("sec", "near")
F32 = jnp.float32
BF16 = jnp.bfloat16


def gelu(x):
    half = 0.5 * x
    return half + half * jnp.tanh(x * (0.7978845608028654 + 0.035677408136300125 * (x * x)))


def normalised(values, axis):
    centred = values - jnp.mean(values, axis=axis, keepdims=True)
    spread_sq = jnp.mean(centred * centred, axis=axis, keepdims=True)
    return centred * lax.rsqrt(spread_sq + 1e-05)


def in_hbm(value):
    return pltpu.with_memory_space_constraint(value, pltpu.HBM)


def in_vmem(value):
    return pltpu.with_memory_space_constraint(value, pltpu.VMEM)


def whole(shape):
    return pl.BlockSpec(shape, lambda *_: (0,) * len(shape))


def split(index, size):
    if size & (size - 1) == 0:
        return index >> (size.bit_length() - 1), index & (size - 1)
    return lax.div(index, size), lax.rem(index, size)


def pick(plan, want_far, half_ref, target_ref, listed, slots, counts):
    _, halves, nears, capacity = plan

    def none(tile, carry):
        counts[tile] = 0
        return carry

    def step(entry, count):
        target = target_ref[entry]
        rank = counts[target]
        counts[target] = rank + 1
        upper, near = split(target, nears)
        sec, half = split(upper, halves)
        listed[count] = entry
        slots[count] = (sec * nears + near) * capacity + rank
        far = (half != half_ref[0]).astype(jnp.int32)
        return count + (far if want_far else 1 - far)

    lax.fori_loop(0, counts.shape[0], none, 0)
    return lax.fori_loop(0, target_ref.shape[0], step, jnp.int32(0), unroll=4)


def multiply(plan, count, source_ref, block_ref, surface_ref, weights, listed, slots, made, labels, tile, out_ref, sems, tile_sem):
    capacity = plan[3]
    block = weights.shape[1]
    labels[...] = jnp.full_like(labels, -1)
    lane = lax.broadcasted_iota(jnp.int32, (1, labels.shape[1]), 1)

    def copy(at):
        peer, rank = split(slots[at], capacity)
        rows = pl.ds(pl.multiple_of(rank * block, block), block)
        return pltpu.make_async_copy(made.at[at], out_ref.at[peer, rows], sems.at[at])

    def group(size, first):
        for i in range(size):
            entry = listed[first + i]
            rows = pl.ds(pl.multiple_of(source_ref[entry] * block, block), block)
            made[first + i] = jnp.dot(
                weights[entry], surface_ref[rows, :], preferred_element_type=F32
            ).astype(BF16)
            peer, rank = split(slots[first + i], capacity)
            row = labels[pl.ds(peer, 1), :]
            labels[pl.ds(peer, 1), :] = jnp.where(lane == rank, block_ref[entry], row)
        for i in range(size):
            copy(first + i).start()

    def eight(i, carry):
        group(8, i * 8)
        return carry

    def one(i, carry):
        group(1, i)
        return carry

    def drain(i, carry):
        copy(i).wait()
        return carry

    def sixteen(i, carry):
        group(16, i * 16)
        return carry

    full = count >> 3
    lax.fori_loop(0, full >> 1, sixteen, 0)
    lax.fori_loop(full >> 1 << 1, full, eight, 0)
    lax.fori_loop(full * 8, count, one, 0)
    tile[...] = jnp.broadcast_to(labels[...].astype(F32)[:, None, :], tile.shape).astype(BF16)
    told = pltpu.make_async_copy(
        tile, out_ref.at[:, pl.ds(capacity * block, tile.shape[1])], tile_sem
    )
    told.start()
    lax.fori_loop(0, count, drain, 0)
    told.wait()


def remap_scratch(plan, entries, block, features):
    sections, halves, nears, _ = plan
    peers = sections * nears
    return [
        pltpu.SMEM((entries + 1,), jnp.int32),
        pltpu.SMEM((entries + 1,), jnp.int32),
        pltpu.SMEM((sections * halves * nears,), jnp.int32),
        pltpu.VMEM((entries, block, block), BF16),
        pltpu.VMEM((entries, block, features), BF16),
        pltpu.VMEM((peers, 128), jnp.int32),
        pltpu.VMEM((peers, 16, features), BF16),
        pltpu.SemaphoreType.DMA((entries,)),
        pltpu.SemaphoreType.DMA,
        pltpu.SemaphoreType.DMA,
    ]


def atm_kernel(
    plan,
    half_ref,
    target_ref,
    source_ref,
    block_ref,
    x_ref,
    gain_ref,
    up_ref,
    down_ref,
    flux_ref,
    weight_ref,
    next_ref,
    surface_ref,
    far_ref,
    normed,
    total,
    listed,
    slots,
    counts,
    weights,
    made,
    labels,
    tile,
    sems,
    tile_sem,
    weight_sem,
):
    step = pl.program_id(0)
    last = step == pl.num_programs(0) - 1
    parts = [slice(at, at + x_ref.shape[0] // 2) for at in (0, x_ref.shape[0] // 2)]
    fetch = pltpu.make_async_copy(weight_ref, weights, weight_sem)

    @pl.when(step == 0)
    def _():
        for rows in parts:
            values = x_ref[rows, :].astype(F32)
            normed[rows, :] = (normalised(values, -1) * gain_ref[...]).astype(BF16)
            total[rows, :] = values

    @pl.when(step == 1)
    def _():
        fetch.start()

    for rows in parts:
        raised = jnp.dot(normed[rows, :], up_ref[...], preferred_element_type=F32)
        hidden = gelu(raised.astype(BF16))
        total[rows, :] += jnp.dot(hidden, down_ref[...], preferred_element_type=F32)

    @pl.when(last)
    def _():
        for rows in parts:
            updated = total[rows, :].astype(BF16)
            next_ref[rows, :] = updated
            surface_ref[rows, :] = jnp.dot(
                updated, flux_ref[...], preferred_element_type=F32
            ).astype(BF16)
        count = pick(plan, True, half_ref, target_ref, listed, slots, counts)
        fetch.wait()
        multiply(plan, count, source_ref, block_ref, surface_ref, weights, listed, slots, made, labels, tile, far_ref, sems, tile_sem)


def atmosphere(plan, half, target, source, target_block, columns, gain, w_up, w_down, w_flux, weights):
    rows, width = columns.shape
    features = w_flux.shape[1]
    inner = w_up.shape[1]
    entries, block, _ = weights.shape
    part = inner // 4
    peers = plan[0] * plan[2]
    return pl.pallas_call(
        functools.partial(atm_kernel, plan),
        name="atmosphere",
        grid_spec=pltpu.PrefetchScalarGridSpec(
            num_scalar_prefetch=4,
            grid=(inner // part,),
            in_specs=[
                whole((rows, width)),
                whole((1, width)),
                pl.BlockSpec((width, part), lambda i, *_: (0, i)),
                pl.BlockSpec((part, width), lambda i, *_: (i, 0)),
                whole(w_flux.shape),
                pl.BlockSpec(memory_space=pltpu.HBM),
            ],
            out_specs=[
                whole((rows, width)),
                whole((rows, features)),
                pl.BlockSpec(memory_space=pltpu.HBM),
            ],
            scratch_shapes=[
                pltpu.VMEM((rows, width), BF16),
                pltpu.VMEM((rows, width), F32),
                *remap_scratch(plan, entries, block, features),
            ],
        ),
        out_shape=[
            pltpu.HBM((rows, width), BF16),
            pltpu.HBM((rows, features), BF16),
            pltpu.HBM((peers, plan[3] * block + 16, features), BF16),
        ],
        compiler_params=pltpu.CompilerParams(vmem_limit_bytes=56 << 20),
    )(
        half,
        target,
        source,
        target_block,
        in_hbm(columns),
        in_hbm(gain[None, :]),
        in_hbm(w_up),
        in_hbm(w_down),
        in_hbm(w_flux),
        in_hbm(weights),
    )


def near_kernel(
    plan,
    half_ref,
    target_ref,
    source_ref,
    block_ref,
    surface_ref,
    weight_ref,
    near_ref,
    listed,
    slots,
    counts,
    weights,
    made,
    labels,
    tile,
    sems,
    tile_sem,
    weight_sem,
):
    fetch = pltpu.make_async_copy(weight_ref, weights, weight_sem)
    fetch.start()
    count = pick(plan, False, half_ref, target_ref, listed, slots, counts)
    fetch.wait()
    multiply(plan, count, source_ref, block_ref, surface_ref, weights, listed, slots, made, labels, tile, near_ref, sems, tile_sem)


def near_remap(plan, half, target, source, target_block, surface, weights):
    entries, block, _ = weights.shape
    features = surface.shape[1]
    peers = plan[0] * plan[2]
    return pl.pallas_call(
        functools.partial(near_kernel, plan),
        name="near_remap",
        grid_spec=pltpu.PrefetchScalarGridSpec(
            num_scalar_prefetch=4,
            grid=(1,),
            in_specs=[whole(surface.shape), pl.BlockSpec(memory_space=pltpu.HBM)],
            out_specs=pl.BlockSpec(memory_space=pltpu.HBM),
            scratch_shapes=remap_scratch(plan, entries, block, features),
        ),
        out_shape=pltpu.HBM((peers, plan[3] * block + 16, features), BF16),
        compiler_params=pltpu.CompilerParams(vmem_limit_bytes=48 << 20),
    )(half, target, source, target_block, in_hbm(surface), in_hbm(weights))


def merge_kernel(capacity, arrived_ref, out_ref, arrived, tile, listed, labels, total, sems, tile_sem):
    peers = arrived.shape[0]
    block = out_ref.shape[1]

    def fetch(peer):
        return pltpu.make_async_copy(
            arrived_ref.at[peer, pl.ds(0, capacity * block)], arrived.at[peer], sems.at[peer]
        )

    told = pltpu.make_async_copy(
        arrived_ref.at[:, pl.ds(capacity * block, tile.shape[1])], tile, tile_sem
    )
    told.start()
    for peer in range(peers):
        fetch(peer).start()
    total[...] = jnp.zeros_like(total)
    told.wait()
    listed[...] = jnp.max(tile[...].astype(F32), axis=1).astype(jnp.int32)
    read = pltpu.make_async_copy(listed, labels, tile_sem)
    read.start()
    read.wait()

    def add(peer, carry):
        fetch(peer).wait()
        for rank in range(capacity):
            label = labels[peer, rank]

            @pl.when(label >= 0)
            def _():
                total[label] += arrived[peer, rank * block : (rank + 1) * block].astype(F32)

        return carry

    lax.fori_loop(0, peers, add, 0)
    out_ref[...] = total[...].astype(BF16)


def merged(capacity, arrived, blocks, block):
    peers, _, features = arrived.shape
    return pl.pallas_call(
        functools.partial(merge_kernel, capacity),
        name="merge",
        grid=(1,),
        in_specs=[pl.BlockSpec(memory_space=pltpu.HBM)],
        out_specs=whole((blocks, block, features)),
        scratch_shapes=[
            pltpu.VMEM((peers, capacity * block, features), BF16),
            pltpu.VMEM((peers, 16, features), BF16),
            pltpu.VMEM((peers, features), jnp.int32),
            pltpu.SMEM((peers, features), jnp.int32),
            pltpu.VMEM((blocks, block, features), F32),
            pltpu.SemaphoreType.DMA((peers,)),
            pltpu.SemaphoreType.DMA,
        ],
        out_shape=jax.ShapeDtypeStruct((blocks, block, features), BF16),
        compiler_params=pltpu.CompilerParams(vmem_limit_bytes=32 << 20),
    )(in_hbm(arrived))


def ocean_kernel(mix_ref, near_ref, far_ref, now_ref, sea_ref, force_ref, gain_ref, up_ref, down_ref, out_ref):
    forcing = (near_ref[...].astype(F32) + far_ref[...].astype(F32)).astype(BF16)
    driven = mix_ref[...].astype(F32) + lax.dot_general(
        force_ref[...], forcing, (((1,), (1,)), ((), ())), preferred_element_type=F32
    )
    normed = (normalised(driven, 0) * gain_ref[...]).astype(BF16)
    hidden = gelu(jnp.dot(up_ref[...], normed, preferred_element_type=F32).astype(BF16))
    change = jnp.dot(down_ref[...], hidden, preferred_element_type=F32)
    out_ref[...] = (
        now_ref[...].astype(F32) + sea_ref[...].astype(F32) * change
    ).astype(BF16)


def ocean(mixing, near, far, now, sea, w_force, gain, w_up, w_down):
    channels, cells = now.shape
    features = near.shape[1]
    part = cells // 3
    if part % 128:
        part = cells
    tall = pl.BlockSpec((channels, part), lambda i: (0, i))
    flat = pl.BlockSpec((part, features), lambda i: (i, 0))
    return pl.pallas_call(
        ocean_kernel,
        name="ocean",
        grid=(cells // part,),
        in_specs=[
            tall,
            flat,
            flat,
            tall,
            pl.BlockSpec((1, part), lambda i: (0, i)),
            whole(w_force.shape),
            whole((channels, 1)),
            whole(w_up.shape),
            whole(w_down.shape),
        ],
        out_specs=tall,
        out_shape=jax.ShapeDtypeStruct((channels, cells), BF16),
        compiler_params=pltpu.CompilerParams(vmem_limit_bytes=32 << 20),
    )(
        in_vmem(mixing),
        in_vmem(near),
        in_vmem(far),
        in_vmem(now),
        in_vmem(sea[None, :]),
        in_vmem(w_force),
        in_vmem(gain),
        in_vmem(w_up),
        in_vmem(w_down),
    )


def exchanged(row, start):
    count = math.prod(lax.axis_size(axis) for axis in ALL)
    pairs = [(i, i + 1) for i in range(start, count - 1, 2)]
    return lax.ppermute(row, ALL, pairs + [(upper, lower) for lower, upper in pairs])


def row_mixing(row, taps):
    row = row.astype(F32)
    return sum(taps[:, step : step + 1] * jnp.roll(row, 1 - step, axis=1) for step in range(3))


def flat_mixing(padded_flat, kernel, row_len, cell_count):
    extended = jnp.pad(padded_flat.astype(F32), ((0, 0), (row_len, row_len)))
    column_at = (jnp.arange(cell_count, dtype=jnp.int32) % row_len)[None, :]
    first_col = column_at == 0
    last_col = column_at == row_len - 1

    def window(offset):
        return lax.slice_in_dim(extended, row_len + offset, row_len + offset + cell_count, axis=1)

    summed = jnp.zeros((padded_flat.shape[0], cell_count), F32)
    for row_step in range(3):
        base = row_step * row_len
        for col_step in range(3):
            if col_step == 0:
                shifted = jnp.where(first_col, window(base + row_len - 1), window(base - 1))
            elif col_step == 2:
                shifted = jnp.where(last_col, window(base - row_len + 1), window(base + 1))
            else:
                shifted = window(base)
            summed = summed + kernel[:, 3 * row_step + col_step][:, None] * shifted
    return summed


def local(
    atm_state,
    gain_atm,
    w_up_atm,
    w_down_atm,
    w_flux,
    ent_source,
    ent_target,
    ent_block,
    remap_weights,
    ocean_state,
    land_sea,
    conv_kernel,
    w_force,
    gain_ocn,
    w_up_ocn,
    w_down_ocn,
):
    sections, halves, nears = (lax.axis_size(axis) for axis in ALL)
    half = lax.axis_index("half")
    peers = sections * nears
    entries, block_rows, _ = remap_weights.shape
    capacity = max(2, 2 * entries // (peers * halves))
    cell_count = ocean_state.shape[1]
    ocean_blocks = cell_count // block_rows

    def exchange(values):
        return lax.all_to_all(values, PEERS, split_axis=0, concat_axis=0, tiled=True)

    plan = (sections, halves, nears, capacity)
    entry = (half[None], ent_target[:, 0], ent_source, ent_block)
    atm_next, surface, far_made = atmosphere(
        plan, *entry, atm_state, gain_atm, w_up_atm, w_down_atm, w_flux, remap_weights
    )
    even = (lax.axis_index(ALL) & 1) == 0
    first, last = ocean_state[:, :OX], ocean_state[:, -OX:]
    across = exchanged(jnp.where(even, first, last), 1)
    far_made, across, later_state = lax.optimization_barrier((far_made, across, ocean_state))
    far_arrived = exchange(far_made)
    near_made = near_remap(plan, *entry, surface, remap_weights)
    none = jnp.zeros_like(across)
    low, high = jnp.where(even, across, none), jnp.where(even, none, across)
    padded = jnp.concatenate([low, ocean_state, high], axis=1)
    mixing = flat_mixing(padded, conv_kernel, OX, cell_count)
    beside = jnp.where(even, later_state[:, -OX:], later_state[:, :OX])
    taps = jnp.where(even, conv_kernel[:, 6:9], conv_kernel[:, 0:3])
    ocean_weights = (w_force.T, gain_ocn[:, None], w_up_ocn.T, w_down_ocn.T)
    far_arrived, near_made, mixing, beside, taps, ocean_weights = lax.optimization_barrier(
        (far_arrived, near_made, mixing, beside, taps, ocean_weights)
    )
    near_arrived = exchange(near_made)
    beside = exchanged(beside, 0)
    far_sum = merged(capacity, far_arrived, ocean_blocks, block_rows)
    far_sum = lax.ppermute(far_sum, "half", [(0, 1), (1, 0)])
    added = row_mixing(beside, taps)
    rest = cell_count - OX
    mixing = (
        mixing
        + jnp.pad(jnp.where(even, 0.0, added), ((0, 0), (0, rest)))
        + jnp.pad(jnp.where(even, added, 0.0), ((0, 0), (rest, 0)))
    ).astype(BF16)
    near_arrived, mixing = lax.optimization_barrier((near_arrived, mixing))
    near_sum = merged(capacity, near_arrived, ocean_blocks, block_rows)
    features = far_sum.shape[2]
    ocean_next = ocean(
        mixing,
        near_sum.reshape(cell_count, features),
        far_sum.reshape(cell_count, features),
        ocean_state,
        land_sea,
        *ocean_weights,
    )
    return (atm_next, ocean_next)


def solution(mesh):
    sections, tiles = mesh.shape["sec"], mesh.shape["tile"]
    fine = Mesh(mesh.devices.reshape(sections, 2, tiles // 2), ALL)
    placed = (
        P(ALL, None),
        P(),
        P(),
        P(),
        P(),
        P(ALL),
        P(ALL, None),
        P(ALL),
        P(ALL, None, None),
        P(None, ALL),
        P(ALL),
        P(),
        P(),
        P(),
        P(),
        P(),
    )
    return jax.shard_map(
        local,
        mesh=fine,
        in_specs=placed,
        out_specs=(P(ALL, None), P(None, ALL)),
        check_vma=False,
    )
```
